128 devices in a mesh: row: 8 (over z, core), col: 16 (over x, y).
Axes of the slice: x: 4, y: 4, z: 4, core: 2. Of those that a mesh axis runs over, the one named last changes fastest.
Arguments:
- rhs_atlas: float32 [65536, 4096], P('row', 'col'), may hold values from -6 to 6
- tile_block: int32 [128], replicated, may hold values from 0 to 127, as said below
- panels: float32 [2, 512, 65536], P(None, 'col', 'row'), may hold values from -0.1875 to 0.1875
- diag_inverse: float32 [2, 512, 512], replicated, as said below
Outputs:
- solved: float32 [2, 512, 4096], P(None, None, 'col')
- trailing: float32 [65536, 4096], P('row', 'col')
The draws below stay inside these ranges and needn't reach their ends.
Inputs may be any that keep to these rules, and one draw needn't show every extreme that they name: tile_block is a permutation of 0 to 127, and each aligned block of 16 entries holds exactly 2 entries of every residue modulo 8. `diag_inverse`: each matrix is lower triangular with diagonal entries between 0.5 and 1.5.
All inputs are finite; a program needn't handle non-finite values.
Results may differ from the reference program's by a relative error of at most 0.00008.
Values sent between devices are 32-bit elements; how exact they have to be, the bound alone decides.
A program may use at most 128 MiB of HBM per device.

```python
import math
import jax
import jax.numpy as jnp
from jax import lax

NB = 512
NRHS = 4096
MB_DEV = 16
M = 65536
N_ROW = 8


def draw_tile_block(key, part):
    share = MB_DEV // N_ROW
    source_keys = jax.random.split(jax.random.fold_in(key, 11), N_ROW)
    places = jax.vmap(lambda k: jax.random.permutation(k, MB_DEV))(source_keys)
    target = places // share
    within = places % share
    target_keys = jax.random.split(jax.random.fold_in(key, 12), N_ROW)
    shuffle = jax.vmap(lambda k: jax.random.permutation(k, MB_DEV))(target_keys)
    source = jnp.arange(N_ROW, dtype=jnp.int32)[:, None]
    local_block = shuffle[target, source * share + within]
    return (local_block * N_ROW + target).reshape(-1).astype(jnp.int32)


def draw_diag_inverse(key, part):
    key_off = jax.random.fold_in(key, 21)
    key_diag = jax.random.fold_in(key, 22)
    rows = jnp.arange(NB)[:, None]
    columns = jnp.arange(NB)[None, :]
    off = jax.random.normal(key_off, (2, NB, NB), jnp.float32)
    diag = jax.random.uniform(key_diag, (2, NB), jnp.float32, 0.6, 1.4)
    below = jnp.where(columns < rows, off / math.sqrt(NB), 0.0)
    on_diag = jnp.where(columns == rows, diag[:, :, None], 0.0)
    return (below + on_diag).astype(jnp.float32)


def levels(own_key, shape, cuts, least, largest):
    factor_of = 1.0
    for position, shards_of in cuts:
        heights = jax.random.uniform(jax.random.fold_in(jax.random.fold_in(own_key, 6), position), (shards_of,), jnp.float32, least / len(cuts), largest / len(cuts))
        factor_of = factor_of * jnp.repeat(jnp.exp(heights), shape[position] // shards_of).reshape((-1,) + (1,) * (len(shape) - 1 - position))
    return factor_of


def bell_draw(own_key, extent, spread, most, cuts=(), kind=jnp.bfloat16):
    factor_of = levels(own_key, extent, cuts, -0.22, 0.18) if cuts else 1.0
    array = jax.random.normal(own_key, extent, jnp.float32) * spread * factor_of
    return jnp.minimum(jnp.maximum(array, -most), most).astype(kind)


def setup_inputs(seed: int = 0) -> dict:
    key_list = jax.random.split(jax.random.key(seed), 5)
    return {
        "rhs_atlas": bell_draw(key_list[0], (M, NRHS), 1.0, 6.0, ((0, 8), (1, 16)), jnp.float32),
        "tile_block": draw_tile_block(jax.random.fold_in(key_list[4], 71), 0),
        "panels": bell_draw(key_list[2], (2, NB, M), (2 * NB) ** -0.5, 0.1875, ((1, 16), (2, 8)), jnp.float32),
        "diag_inverse": draw_diag_inverse(jax.random.fold_in(key_list[4], 71), 0),
    }


def reference(rhs_atlas, tile_block, panels, diag_inverse):
    highest = lax.Precision.HIGHEST
    count = MB_DEV * N_ROW
    tiles = rhs_atlas.reshape(count, NB, NRHS)
    order = jnp.argsort(tile_block).astype(jnp.int32)
    rhs = jnp.take(tiles, order, axis=0)
    block_ids = jnp.arange(count, dtype=jnp.int32)
    slot = (block_ids % N_ROW) * MB_DEV + block_ids // N_ROW

    def lower(which):
        pan = panels[which].reshape(NB, count, NB)
        pan = jnp.take(pan, slot, axis=1)
        return jnp.transpose(pan, (1, 2, 0)).reshape(count * NB, NB)

    first = jnp.dot(diag_inverse[0], rhs[0], precision=highest, preferred_element_type=jnp.float32)
    update = jnp.dot(lower(0), first, precision=highest, preferred_element_type=jnp.float32).reshape(count, NB, NRHS)
    rhs = rhs - jnp.where((block_ids >= 1)[:, None, None], update, jnp.float32(0.0))
    second = jnp.dot(diag_inverse[1], rhs[1], precision=highest, preferred_element_type=jnp.float32)
    update = jnp.dot(lower(1), second, precision=highest, preferred_element_type=jnp.float32).reshape(count, NB, NRHS)
    rhs = rhs - jnp.where((block_ids >= 2)[:, None, None], update, jnp.float32(0.0))
    slots = jnp.arange(count, dtype=jnp.int32)
    block_of_slot = (slots % MB_DEV) * N_ROW + slots // MB_DEV
    trailing = jnp.take(rhs, block_of_slot, axis=0).reshape(count * NB, NRHS)
    return jnp.stack([first, second]), trailing
```

```python
import jax
import jax.numpy as jnp
from jax import lax
from jax.experimental import pallas as pl
from jax.experimental.pallas import tpu as pltpu
from jax.sharding import PartitionSpec as P

MESH = pl.DeviceIdType.MESH
F32 = jnp.float32
BF16 = jnp.bfloat16
NB = 512
W = 256
ROWS = 8
TILES = 16
Q = 4


def split(v):
    hi = v.astype(BF16)
    return hi, (v - hi.astype(F32)).astype(BF16)


def dot_t(a, b):
    return lax.dot_general(
        a, b, (((0,), (0,)), ((), ())), precision=lax.Precision.HIGHEST, preferred_element_type=F32
    )


def exchange(
    idx, rhs, panels, dinv,
    recv, upd, solved,
    rhs_v, send_v, lg, sg, sh, sl, lh, ll, ub, mm, xb, rs, rr, b1, dv, first_n,
    loc, b1z_s, b1z_r, b1g_s, b1g_r, b1o_s, b1o_r, lg_s, lg_r, lo_s, lo_r,
    mx_s, mx_r, rs_s, rs_r, ag_s, ag_r, rx_s, rx_r, az_s, az_r, sg_s, sg_r, u_s, u_r, u_l,
):
    row = lax.axis_index("row")
    col = lax.axis_index("col")
    z, core = row // 2, row % 2
    x, y = col // Q, col % Q
    g = x + core * (y - x)
    o = y + core * (x - y)

    def col_of(gg, oo):
        return gg * Q + oo + core * ((oo * Q + gg) - (gg * Q + oo))

    def at_g(d):
        return (row, col_of((g + d) % Q, o))

    def at_o(d):
        return (row, col_of(g, (o + d) % Q))

    def at_z(d):
        return (((z + d) % Q) * 2 + core, col)

    def at_row(d):
        return ((row + d) % ROWS, col)

    sibling = (z * 2 + 1 - core, col)

    def remote(src, dst, ss, rsem, dev):
        return pltpu.make_async_remote_copy(
            src_ref=src, dst_ref=dst, send_sem=ss, recv_sem=rsem, device_id=dev, device_id_type=MESH
        )

    def landed(ref, ss, rsem, dev):
        remote(ref, ref, ss, rsem, dev).wait_recv()

    rhs_in = pltpu.make_async_copy(rhs, rhs_v, loc.at[0])
    rhs_in.start()
    dinv_in = pltpu.make_async_copy(dinv, dv, loc.at[1])
    dinv_in.start()

    def quarter(gg):
        return panels.at[:, :, pl.ds(pl.multiple_of(gg * (Q * NB), Q * NB), Q * NB)]

    own_l = pltpu.make_async_copy(quarter(g), lg.at[:, o, g], loc.at[2])
    own_l.start()

    barrier = pltpu.get_barrier_semaphore()
    for d in range(1, ROWS):
        pl.semaphore_signal(barrier, inc=1, device_id=at_row(d), device_id_type=MESH)
    for d in range(1, Q):
        pl.semaphore_signal(barrier, inc=1, device_id=at_g(d), device_id_type=MESH)
        pl.semaphore_signal(barrier, inc=1, device_id=at_o(d), device_id_type=MESH)
    pl.semaphore_wait(barrier, ROWS - 1 + 2 * (Q - 1))

    head = panels.at[0, :, pl.ds(0, NB)]

    @pl.when(row == 1)
    def _():
        for d in range(1, ROWS):
            r2 = (row + d) % ROWS
            c2 = r2 % 2
            g2 = x + c2 * (y - x)
            o2 = y + c2 * (x - y)
            remote(head, b1.at[o2, g2], b1z_s.at[d - 1], b1z_r, (r2, col)).start()
        own = pltpu.make_async_copy(head, b1.at[o, g], loc.at[3])
        own.start()
        own.wait()

    lg_c = []
    for d in range(1, Q):
        c = remote(quarter((g + d) % Q), lg.at[:, o, g], lg_s.at[d - 1], lg_r.at[d - 1], at_g(d))
        c.start()
        lg_c.append(c)

    rhs_in.wait()
    for p in range(2):
        held = idx[TILES + 2 * p + 1].astype(F32)
        mm[p] = rhs_v[idx[TILES + 2 * p]] * held
    half = pl.multiple_of(core * W, W)
    other = pl.multiple_of((1 - core) * W, W)
    mx = remote(mm.at[:, pl.ds(other, W)], xb, mx_s, mx_r, sibling)
    mx.start()

    def reorder(t, carry):
        send_v[t] = rhs_v[idx[t]]
        return carry

    lax.fori_loop(0, TILES, reorder, 0)

    @pl.when(row != 1)
    def _():
        landed(b1.at[o, g], b1z_s.at[0], b1z_r, (1, col))

    b1g_c = []
    for d in range(1, Q):
        c = remote(b1.at[o, g], b1.at[o, g], b1g_s.at[d - 1], b1g_r.at[d - 1], at_g(d))
        c.start()
        b1g_c.append(c)

    mx.wait()
    mm[:, pl.ds(half, W)] = mm[:, pl.ds(half, W)] + xb[...]

    def piece(zz):
        return pl.ds(pl.multiple_of(half + zz * (W // Q), W // Q), W // Q)

    rs_c = []
    for d in range(1, Q):
        c = remote(mm.at[:, piece((z + d) % Q)], rs.at[d - 1], rs_s.at[d - 1], rs_r.at[d - 1], at_z(d))
        c.start()
        rs_c.append(c)

    for d in range(1, Q):
        landed(b1.at[o, (g + Q - d) % Q], b1g_s.at[d - 1], b1g_r.at[d - 1], at_g(d))
    b1o_c = []
    for d in range(1, Q):
        c = remote(b1.at[o], b1.at[o], b1o_s.at[d - 1], b1o_r.at[d - 1], at_o(d))
        c.start()
        b1o_c.append(c)

    for d in range(1, Q):
        landed(rs.at[d - 1], rs_s.at[d - 1], rs_r.at[d - 1], at_z(d))
    mine = piece(z)
    rr[:, mine] = mm[:, mine] + (rs[0] + rs[1] + rs[2])
    ag_c = []
    for d in range(1, Q):
        c = remote(rr.at[:, mine], rr.at[:, mine], ag_s.at[d - 1], ag_r.at[d - 1], at_z(d))
        c.start()
        ag_c.append(c)

    az_c = []
    for d in (2, 4, 6, 1, 3, 5, 7):
        c = remote(
            send_v.at[pl.ds(2 * ((row + d) % ROWS), 2)], recv.at[pl.ds(2 * row, 2)],
            az_s.at[d - 1], az_r.at[d - 1], at_row(d),
        )
        c.start()
        az_c.append(c)
    own_t = pltpu.make_async_copy(send_v.at[pl.ds(2 * row, 2)], recv.at[pl.ds(2 * row, 2)], loc.at[4])
    own_t.start()

    own_l.wait()
    for d in range(1, Q):
        landed(lg.at[:, o, (g + Q - d) % Q], lg_s.at[d - 1], lg_r.at[d - 1], at_g(d))
    lo_c = []
    for n, d in enumerate((1, Q - 1)):
        c = remote(lg.at[:, o], lg.at[:, o], lo_s.at[n], lo_r.at[n], at_o(d))
        c.start()
        lo_c.append(c)

    for d in range(1, Q):
        landed(rr.at[:, piece((z + Q - d) % Q)], ag_s.at[d - 1], ag_r.at[d - 1], at_z(d))
    rx = remote(rr.at[:, pl.ds(half, W)], rr.at[:, pl.ds(half, W)], rx_s, rx_r, sibling)
    rx.start()
    dinv_in.wait()
    rx.wait_send()
    landed(rr.at[:, pl.ds(other, W)], rx_s, rx_r, sibling)

    def arrange(which, value):
        first_n[...] = value
        solved[which] = value

        def put(n, carry):
            oo, gg = n // Q, n % Q
            sg[g, which, pl.ds(pl.multiple_of(n * 32, 32), 32)] = first_n[
                pl.ds(pl.multiple_of(col_of(gg, oo) * 32, 32), 32)
            ]
            return carry

        lax.fori_loop(0, TILES, put, 0)

    sg_c = []

    def spread(which):
        for d in (2, 1, 3):
            n = which * (Q - 1) + d - 1
            c = remote(sg.at[g, which], sg.at[g, which], sg_s.at[n], sg_r.at[n], at_g(d))
            c.start()
            sg_c.append(c)

    def solve(which, block):
        return jnp.dot(dv[which], block, precision=lax.Precision.HIGHEST, preferred_element_type=F32)

    arrange(0, solve(0, rr[0]))
    spread(0)
    for d in range(1, Q):
        landed(b1.at[(o + Q - d) % Q], b1o_s.at[d - 1], b1o_r.at[d - 1], at_o(d))
    reduced = rr[1] - dot_t(b1[...].reshape(NB, NB), sg[g, 0])
    arrange(1, solve(1, reduced))
    spread(1)

    landed(lg.at[:, (o + Q - 1) % Q], lo_s.at[0], lo_r.at[0], at_o(1))
    c = remote(lg.at[0, (o + Q - 1) % Q], lg.at[0, (o + Q - 1) % Q], lo_s.at[2], lo_r.at[2], at_o(1))
    c.start()
    lo_c.append(c)
    landed(lg.at[:, (o + 1) % Q], lo_s.at[1], lo_r.at[1], at_o(Q - 1))
    c = remote(lg.at[1, (o + 1) % Q], lg.at[1, (o + 1) % Q], lo_s.at[3], lo_r.at[3], at_o(Q - 1))
    c.start()
    lo_c.append(c)

    def split_solved(gg):
        for p in range(2):
            hi, lo = split(sg[gg, p])
            sh[gg, pl.ds(p * NB, NB)] = hi
            sl[gg, pl.ds(p * NB, NB)] = lo

    split_solved(g)
    for d in range(1, Q):
        gg = (g + Q - d) % Q
        for p in range(2):
            n = p * (Q - 1) + d - 1
            landed(sg.at[gg, p], sg_s.at[n], sg_r.at[n], at_g(d))
        split_solved(gg)

    landed(lg.at[0, (o + 2) % Q], lo_s.at[2], lo_r.at[2], at_o(1))
    landed(lg.at[1, (o + 2) % Q], lo_s.at[3], lo_r.at[3], at_o(Q - 1))

    def tile_step(i, carry):
        def turn(n, inner):
            p = n // Q
            keep = jnp.where((i == 0) & (g == 0) & (row <= p), 0.0, 1.0).astype(F32)
            part = lg[p, n % Q, :, :, pl.ds(pl.multiple_of(i * NB, NB), NB)].reshape(4 * 32, NB)
            hi, lo = split(part.T * keep)
            at = pl.ds(pl.multiple_of(n * 128, 128), 128)
            lh[:, at] = hi
            ll[:, at] = lo
            return inner

        lax.fori_loop(0, 2 * Q, turn, 0)

        def dest_step(m, inner):
            d = (m + 2) % Q
            gg = (g + d) % Q
            a, b = lh[...], sh[gg]
            acc = jnp.dot(a, b, preferred_element_type=F32)
            acc += jnp.dot(a, sl[gg], preferred_element_type=F32)
            acc += jnp.dot(ll[...], b, preferred_element_type=F32)
            ub[d, i] = acc

            @pl.when(d != 0)
            def _():
                remote(ub.at[d, i], upd.at[Q * g + i], u_s.at[d, i], u_r.at[d, i], (row, col_of(gg, o))).start()

            @pl.when(d == 0)
            def _():
                pltpu.make_async_copy(ub.at[d, i], upd.at[Q * g + i], u_l.at[i]).start()

            return inner

        lax.fori_loop(0, Q, dest_step, 0)
        return carry

    lax.fori_loop(0, Q, tile_step, 0)

    for i in range(Q):
        pltpu.make_async_copy(ub.at[0, i], upd.at[Q * g + i], u_l.at[i]).wait()
        for d in range(1, Q):
            remote(ub.at[d, i], upd.at[Q * g + i], u_s.at[d, i], u_r.at[d, i], at_g(d)).wait_send()
            landed(upd.at[Q * ((g + Q - d) % Q) + i], u_s.at[d, i], u_r.at[d, i], at_g(d))
    own_t.wait()
    for c in az_c:
        c.wait_send()
    for d in range(1, ROWS):
        landed(recv.at[pl.ds(2 * ((row + ROWS - d) % ROWS), 2)], az_s.at[d - 1], az_r.at[d - 1], at_row(d))
    for c in lg_c + b1g_c + b1o_c + rs_c + ag_c + lo_c + sg_c:
        c.wait_send()

    @pl.when(row == 1)
    def _():
        for d in range(1, ROWS):
            remote(head, b1.at[o, g], b1z_s.at[d - 1], b1z_r, at_row(d)).wait_send()


def finish_body(placing, tile, update, out):
    out[...] = tile[...] - update[...]


def shards(rhs_atlas, tile_block, panels, diag_inverse):
    me = lax.axis_index("row")
    every = jnp.arange(ROWS * TILES, dtype=jnp.int32)
    local = jnp.arange(TILES, dtype=jnp.int32)
    target = tile_block % ROWS
    mine = lax.dynamic_slice_in_dim(target, me * TILES, TILES)
    earlier = (mine[None, :] == mine[:, None]) & (local[None, :] < local[:, None])
    rank = 2 * mine + jnp.sum(earlier.astype(jnp.int32), axis=1)
    order = jnp.sum(jnp.where(rank[None, :] == local[:, None], local[None, :], 0), axis=1)
    where_is = jnp.sum(jnp.where(tile_block[None, :] == (local * ROWS + me)[:, None], every[None, :], 0), axis=1)
    before = (every[None, :] < where_is[:, None]) & (target == me)[None, :]
    placing = jnp.sum(before.astype(jnp.int32), axis=1)
    lead = jnp.sum(jnp.where(tile_block[None, :] == jnp.arange(2, dtype=jnp.int32)[:, None], every[None, :], 0), axis=1)
    lead = jnp.stack([lead % TILES, (lead // TILES == me).astype(jnp.int32)], axis=1).reshape(4)
    idx = jnp.concatenate([order, lead])

    dma = pltpu.SemaphoreType.DMA
    hbm = pl.BlockSpec(memory_space=pltpu.HBM)
    recv, upd, solved = pl.pallas_call(
        exchange,
        out_shape=(
            jax.ShapeDtypeStruct((TILES, NB, W), F32),
            jax.ShapeDtypeStruct((TILES, NB, W), F32),
            jax.ShapeDtypeStruct((2, NB, W), F32),
        ),
        in_specs=[pl.BlockSpec(memory_space=pltpu.SMEM), hbm, hbm, hbm],
        out_specs=(hbm, hbm, pl.BlockSpec(memory_space=pltpu.VMEM)),
        scratch_shapes=[
            pltpu.VMEM((TILES, NB, W), F32),
            pltpu.VMEM((TILES, NB, W), F32),
            pltpu.VMEM((2, Q, Q, 32, Q * NB), F32),
            pltpu.VMEM((Q, 2, NB, W), F32),
            pltpu.VMEM((Q, 2 * NB, W), BF16),
            pltpu.VMEM((Q, 2 * NB, W), BF16),
            pltpu.VMEM((NB, 2 * NB), BF16),
            pltpu.VMEM((NB, 2 * NB), BF16),
            pltpu.VMEM((Q, Q, NB, W), F32),
            pltpu.VMEM((2, NB, W), F32),
            pltpu.VMEM((2, W, W), F32),
            pltpu.VMEM((Q - 1, 2, W // Q, W), F32),
            pltpu.VMEM((2, NB, W), F32),
            pltpu.VMEM((Q, Q, 32, NB), F32),
            pltpu.VMEM((2, NB, NB), F32),
            pltpu.VMEM((NB, W), F32),
            dma((5,)),
            dma((7,)), dma(()), dma((3,)), dma((3,)), dma((3,)), dma((3,)),
            dma((3,)), dma((3,)), dma((4,)), dma((4,)),
            dma(()), dma(()), dma((3,)), dma((3,)), dma((3,)), dma((3,)), dma(()), dma(()),
            dma((7,)), dma((7,)), dma((6,)), dma((6,)),
            dma((Q, Q)), dma((Q, Q)), dma((Q,)),
        ],
        compiler_params=pltpu.CompilerParams(
            collective_id=0, has_side_effects=True, vmem_limit_bytes=60 * 1024 * 1024
        ),
        name="exchange",
    )(idx, rhs_atlas.reshape(TILES, NB, W), panels, diag_inverse)

    block = (None, NB, W)
    trailing = pl.pallas_call(
        finish_body,
        grid_spec=pltpu.PrefetchScalarGridSpec(
            num_scalar_prefetch=1,
            grid=(TILES,),
            in_specs=[
                pl.BlockSpec(block, lambda b, placing: (placing[b], 0, 0)),
                pl.BlockSpec(block, lambda b, placing: (b, 0, 0)),
            ],
            out_specs=pl.BlockSpec(block, lambda b, placing: (b, 0, 0)),
        ),
        out_shape=jax.ShapeDtypeStruct((TILES, NB, W), F32),
        name="finish",
    )(placing, recv, upd)
    return solved, trailing.reshape(TILES * NB, W)


def solution(mesh):
    placed = (P("row", "col"), P(), P(None, "col", "row"), P())
    return jax.shard_map(
        shards,
        mesh=mesh,
        in_specs=placed,
        out_specs=(P(None, None, "col"), P("row", "col")),
        check_vma=False,
    )
```

```python
import jax
import jax.numpy as jnp
from jax import lax
from jax.experimental import pallas as pl
from jax.experimental.pallas import tpu as pltpu
from jax.sharding import PartitionSpec as P

MESH = pl.DeviceIdType.MESH
F32 = jnp.float32
BF16 = jnp.bfloat16
NB = 512
W = 256
ROWS = 8
TILES = 16
Q = 4


def split(v):
    hi = v.astype(BF16)
    return hi, (v - hi.astype(F32)).astype(BF16)


def dot_t(a, b):
    return lax.dot_general(
        a, b, (((0,), (0,)), ((), ())), precision=lax.Precision.HIGHEST, preferred_element_type=F32
    )


def exchange(
    tb, tbv, rhs, panels, dinv,
    recv, upd, solved, placing,
    rhs_v, send_v, lg, sg, sh, sl, lh, ll, mm, xb, rs, rr, b1, dv, first_n, order,
    loc, b1z_s, b1z_r, b1g_s, b1g_r, b1o_s, b1o_r, lg_s, lg_r, lo_s, lo_r, lf_s, lf_r,
    mx_s, mx_r, rs_s, rs_r, ag_s, ag_r, rx_s, rx_r, hx_s, hx_r, az_s, az_r,
    sg_s, sg_r, sf_s, sf_r, u_s, u_r,
):
    row = lax.axis_index("row")
    col = lax.axis_index("col")
    z, core = row // 2, row % 2
    x, y = col // Q, col % Q
    g = x + core * (y - x)
    o = y + core * (x - y)
    left_g, right_g, far_g = (g + 3) % Q, (g + 1) % Q, (g + 2) % Q
    left_o, right_o, far_o = (o + 3) % Q, (o + 1) % Q, (o + 2) % Q

    def col_of(gg, oo):
        return gg * Q + oo + core * ((oo * Q + gg) - (gg * Q + oo))

    def at_g(d):
        return (row, col_of((g + d) % Q, o))

    def at_o(d):
        return (row, col_of(g, (o + d) % Q))

    def at_z(d):
        return (((z + d) % Q) * 2 + core, col)

    def at_row(d):
        return ((row + d) % ROWS, col)

    sibling = (z * 2 + 1 - core, col)

    def remote(src, dst, ss, rsem, dev):
        return pltpu.make_async_remote_copy(
            src_ref=src, dst_ref=dst, send_sem=ss, recv_sem=rsem, device_id=dev, device_id_type=MESH
        )

    def landed(ref, ss, rsem, dev):
        remote(ref, ref, ss, rsem, dev).wait_recv()

    sent = []

    def send(src, dst, ss, rsem, dev):
        c = remote(src, dst, ss, rsem, dev)
        c.start()
        sent.append(c)

    rhs_in = pltpu.make_async_copy(rhs, rhs_v, loc.at[0])
    rhs_in.start()

    def quarter(p, gg):
        return panels.at[p, :, pl.ds(pl.multiple_of(gg * (Q * NB), Q * NB), Q * NB)]

    own_l = []
    for p in range(2):
        c = pltpu.make_async_copy(quarter(p, g), lg.at[p, o, g], loc.at[1 + p])
        c.start()
        own_l.append(c)
    dinv_in = pltpu.make_async_copy(dinv, dv, loc.at[3])
    dinv_in.start()

    barrier = pltpu.get_barrier_semaphore()
    for d in range(1, ROWS):
        pl.semaphore_signal(barrier, inc=1, device_id=at_row(d), device_id_type=MESH)
    for d in range(1, Q):
        pl.semaphore_signal(barrier, inc=1, device_id=at_g(d), device_id_type=MESH)
        pl.semaphore_signal(barrier, inc=1, device_id=at_o(d), device_id_type=MESH)

    mine = [tb[row * TILES + t] for t in range(TILES)]
    goal = [v % ROWS for v in mine]
    for r in range(ROWS):
        low, high = jnp.int32(0), jnp.int32(0)
        for t in range(TILES):
            high = jnp.where(goal[t] == r, t, high)
            low = jnp.where(goal[TILES - 1 - t] == r, TILES - 1 - t, low)
        order[2 * r] = low
        order[2 * r + 1] = high
    for p in range(2):
        where_p, held = jnp.int32(0), jnp.int32(0)
        for t in range(TILES):
            where_p = jnp.where(mine[t] == p, t, where_p)
            held = jnp.where(mine[t] == p, 1, held)
        order[TILES + 2 * p] = where_p
        order[TILES + 2 * p + 1] = held

    pl.semaphore_wait(barrier, ROWS - 1 + 2 * (Q - 1))

    def head(c2):
        return panels.at[0, :, pl.ds(pl.multiple_of(c2 * W, W), W)]

    @pl.when(row == 1)
    def _():
        for d in range(1, ROWS):
            r2 = (row + d) % ROWS
            c2 = r2 % 2
            g2 = x + c2 * (y - x)
            o2 = y + c2 * (x - y)
            remote(head(c2), b1.at[o2, g2], b1z_s.at[d - 1], b1z_r, (r2, col)).start()
        own = pltpu.make_async_copy(head(core), b1.at[o, g], loc.at[4])
        own.start()
        own.wait()

    for p in range(2):
        for d in (2, 1, 3):
            send(quarter(p, (g + d) % Q), lg.at[p, o, g], lg_s.at[p, d - 1], lg_r.at[p, d - 1], at_g(d))

    rhs_in.wait()
    for p in range(2):
        mm[p] = rhs_v[order[TILES + 2 * p]] * order[TILES + 2 * p + 1].astype(F32)
    half = pl.ds(pl.multiple_of(core * W, W), W)
    other = pl.ds(pl.multiple_of((1 - core) * W, W), W)
    send(mm.at[:, other], xb, mx_s, mx_r, sibling)

    def reorder(t, carry):
        send_v[t] = rhs_v[order[t]]
        return carry

    lax.fori_loop(0, TILES, reorder, 0)

    @pl.when(row != 1)
    def _():
        landed(b1.at[o, g], b1z_s.at[0], b1z_r, (1, col))

    for d in range(1, Q):
        send(b1.at[o, g], b1.at[o, g], b1g_s.at[d - 1], b1g_r.at[d - 1], at_g(d))

    sent.pop(-4).wait_send()
    landed(xb, mx_s, mx_r, sibling)
    mm[:, half] = mm[:, half] + xb[...]

    def piece(zz):
        return pl.ds(pl.multiple_of(core * W + zz * (W // Q), W // Q), W // Q)

    for d in (2, 1, 3):
        send(mm.at[:, piece((z + d) % Q)], rs.at[d - 1], rs_s.at[d - 1], rs_r.at[d - 1], at_z(d))
    pieces = [sent.pop() for _ in range(Q - 1)]

    for d in range(1, Q):
        landed(b1.at[o, (g + Q - d) % Q], b1g_s.at[d - 1], b1g_r.at[d - 1], at_g(d))
    for d in range(1, Q):
        send(b1.at[o], b1.at[o], b1o_s.at[d - 1], b1o_r.at[d - 1], at_o(d))

    for d in range(1, Q):
        landed(rs.at[d - 1], rs_s.at[d - 1], rs_r.at[d - 1], at_z(d))
    rr[:, piece(z)] = mm[:, piece(z)] + (rs[0] + rs[1] + rs[2])
    for d in (2, 1, 3):
        send(rr.at[:, piece(z)], rr.at[:, piece(z)], ag_s.at[d - 1], ag_r.at[d - 1], at_z(d))

    for d in (4, 2, 6, 3, 5, 1, 7):
        send(
            send_v.at[pl.ds(2 * ((row + d) % ROWS), 2)], recv.at[pl.ds(2 * row, 2)],
            az_s.at[d - 1], az_r.at[d - 1], at_row(d),
        )
    own_t = pltpu.make_async_copy(send_v.at[pl.ds(2 * row, 2)], recv.at[pl.ds(2 * row, 2)], loc.at[5])
    own_t.start()

    for p in range(2):
        own_l[p].wait()
        for d in range(1, Q):
            landed(lg.at[p, o, (g + Q - d) % Q], lg_s.at[p, d - 1], lg_r.at[p, d - 1], at_g(d))
        for n, d in ((p, (1, Q - 1)[p]), (1 - p, (Q - 1, 1)[p])):
            send(lg.at[p, o], lg.at[p, o], lo_s.at[p, n], lo_r.at[p, n], at_o(d))

    for d in range(1, Q):
        landed(rr.at[:, piece((z + Q - d) % Q)], ag_s.at[d - 1], ag_r.at[d - 1], at_z(d))
    send(rr.at[:, half], rr.at[:, half], rx_s, rx_r, sibling)
    dinv_in.wait()
    landed(rr.at[:, other], rx_s, rx_r, sibling)

    def arrange(which, value):
        first_n[...] = value
        solved[which] = value

        def put(n, carry):
            oo, gg = n // Q, n % Q
            sg[g, which, pl.ds(pl.multiple_of(n * 32, 32), 32)] = first_n[
                pl.ds(pl.multiple_of(col_of(gg, oo) * 32, 32), 32)
            ]
            return carry

        lax.fori_loop(0, TILES, put, 0)

    def spread(p):
        for n, d in ((p, (1, Q - 1)[p]), (1 - p, (Q - 1, 1)[p])):
            send(sg.at[g, p], sg.at[g, p], sg_s.at[p, n], sg_r.at[p, n], at_g(d))

    def solve(which, block):
        return jnp.dot(dv[which], block, precision=lax.Precision.HIGHEST, preferred_element_type=F32)

    arrange(0, solve(0, rr[0]))
    spread(0)
    for d in range(1, Q):
        landed(b1.at[(o + Q - d) % Q], b1o_s.at[d - 1], b1o_r.at[d - 1], at_o(d))
    for c in pieces:
        c.wait_send()
    mm[0, half] = rr[1, half] - dot_t(b1[...].reshape(NB, W), sg[g, 0])
    send(mm.at[0, half], mm.at[0, half], hx_s, hx_r, sibling)
    landed(mm.at[0, other], hx_s, hx_r, sibling)
    arrange(1, solve(1, mm[0]))
    spread(1)

    def split_solved(gg, p):
        hi, lo = split(sg[gg, p])
        sh[gg, pl.ds(p * NB, NB)] = hi
        sl[gg, pl.ds(p * NB, NB)] = lo

    for p in range(2):
        d = (1, Q - 1)[p]
        oo, gg = ((left_o, left_g), (right_o, right_g))[p]
        landed(lg.at[p, oo], lo_s.at[p, p], lo_r.at[p, p], at_o(d))
        send(lg.at[p, oo], lg.at[p, oo], lf_s.at[p], lf_r.at[p], at_o(d))
        landed(sg.at[gg, p], sg_s.at[p, p], sg_r.at[p, p], at_g(d))
        send(sg.at[gg, p], sg.at[gg, p], sf_s.at[p], sf_r.at[p], at_g(d))
        split_solved(g, p)
        split_solved(gg, p)
    for p in range(2):
        d = (Q - 1, 1)[p]
        oo, gg = ((right_o, right_g), (left_o, left_g))[p]
        landed(lg.at[p, oo], lo_s.at[p, 1 - p], lo_r.at[p, 1 - p], at_o(d))
        landed(sg.at[gg, p], sg_s.at[p, 1 - p], sg_r.at[p, 1 - p], at_g(d))
        split_solved(gg, p)
    for p in range(2):
        landed(sg.at[far_g, p], sf_s.at[p], sf_r.at[p], at_g(1))
        split_solved(far_g, p)
    for p in range(2):
        landed(lg.at[p, far_o], lf_s.at[p], lf_r.at[p], at_o(1))

    def tile_step(i, carry):
        def turn(n, inner):
            p = n // Q
            keep = jnp.where((i == 0) & (g == 0) & (row <= p), 0.0, 1.0).astype(F32)
            part = lg[p, n % Q, :, :, pl.ds(pl.multiple_of(i * NB, NB), NB)].reshape(4 * 32, NB)
            hi, lo = split(part.T * keep)
            at = pl.ds(pl.multiple_of(n * 128, 128), 128)
            lh[:, at] = hi
            ll[:, at] = lo
            return inner

        lax.fori_loop(0, 2 * Q, turn, 0)

        def dest_step(m, inner):
            d = (m + 2) % Q
            gg = (g + d) % Q
            a, b = lh[...], sh[gg]
            acc = jnp.dot(a, b, preferred_element_type=F32)
            acc += jnp.dot(a, sl[gg], preferred_element_type=F32)
            acc += jnp.dot(ll[...], b, preferred_element_type=F32)

            @pl.when(d != 0)
            def _():
                n = Q * d - Q + i
                rhs_v[n] = acc
                remote(rhs_v.at[n], upd.at[Q * g + i], u_s.at[n], u_r.at[n], (row, col_of(gg, o))).start()

            @pl.when(d == 0)
            def _():
                upd[Q * g + i] = acc

            return inner

        lax.fori_loop(0, Q, dest_step, 0)
        return carry

    lax.fori_loop(0, Q, tile_step, 0)

    ids = tbv[...]
    every = lax.broadcasted_iota(jnp.int32, (TILES, ROWS * TILES), 1)
    want = lax.broadcasted_iota(jnp.int32, (TILES, ROWS * TILES), 0) * ROWS + row
    where_is = jnp.sum(jnp.where(ids == want, every, 0), axis=1, keepdims=True)
    before = (every < where_is) & (ids % ROWS == row)
    count = jnp.sum(before.astype(jnp.int32), axis=1, keepdims=True)
    for b in range(TILES):
        placing[b] = count[b, 0]

    own_t.wait()
    for d in range(1, ROWS):
        landed(recv.at[pl.ds(2 * ((row + ROWS - d) % ROWS), 2)], az_s.at[d - 1], az_r.at[d - 1], at_row(d))
    for c in sent:
        c.wait_send()

    @pl.when(row == 1)
    def _():
        for d in range(1, ROWS):
            r2 = (row + d) % ROWS
            remote(head(r2 % 2), b1.at[o, g], b1z_s.at[d - 1], b1z_r, (r2, col)).wait_send()

    for i in range(Q):
        for d in range(1, Q):
            n = Q * d - Q + i
            remote(rhs_v.at[n], upd.at[Q * g + i], u_s.at[n], u_r.at[n], at_g(d)).wait_send()
            landed(upd.at[Q * ((g + Q - d) % Q) + i], u_s.at[n], u_r.at[n], at_g(d))


def finish_body(placing, recv, upd, solved, out, solved_out, stage, sems, sol_sem):
    sol = pltpu.make_async_copy(solved, solved_out, sol_sem)
    sol.start()
    depth = stage.shape[0]

    def put(b):
        return pltpu.make_async_copy(stage.at[b % depth], out.at[b], sems.at[b % depth])

    for b in range(TILES):
        if b >= depth:
            put(b - depth).wait()
        stage[b % depth] = recv[placing[b]] - upd[b]
        put(b).start()
    for b in range(TILES - depth, TILES):
        put(b).wait()
    sol.wait()


def shards(rhs_atlas, tile_block, panels, diag_inverse):
    dma = pltpu.SemaphoreType.DMA
    hbm = pl.BlockSpec(memory_space=pltpu.HBM)
    vmem = pl.BlockSpec(memory_space=pltpu.VMEM)
    smem = pl.BlockSpec(memory_space=pltpu.SMEM)
    tiles = (TILES, NB, W)
    recv, upd, solved, placing = pl.pallas_call(
        exchange,
        out_shape=(
            pltpu.VMEM(tiles, F32),
            pltpu.VMEM(tiles, F32),
            pltpu.VMEM((2, NB, W), F32),
            jax.ShapeDtypeStruct((TILES,), jnp.int32),
        ),
        in_specs=[smem, vmem, hbm, hbm, hbm],
        out_specs=(vmem, vmem, vmem, smem),
        scratch_shapes=[
            pltpu.VMEM(tiles, F32),
            pltpu.VMEM(tiles, F32),
            pltpu.VMEM((2, Q, Q, 32, Q * NB), F32),
            pltpu.VMEM((Q, 2, NB, W), F32),
            pltpu.VMEM((Q, 2 * NB, W), BF16),
            pltpu.VMEM((Q, 2 * NB, W), BF16),
            pltpu.VMEM((NB, 2 * NB), BF16),
            pltpu.VMEM((NB, 2 * NB), BF16),
            pltpu.VMEM((2, NB, W), F32),
            pltpu.VMEM((2, W, W), F32),
            pltpu.VMEM((Q - 1, 2, W // Q, W), F32),
            pltpu.VMEM((2, NB, W), F32),
            pltpu.VMEM((Q, Q, 32, W), F32),
            pltpu.VMEM((2, NB, NB), F32),
            pltpu.VMEM((NB, W), F32),
            pltpu.SMEM((TILES + 4,), jnp.int32),
            dma((6,)),
            dma((7,)), dma(()), dma((3,)), dma((3,)), dma((3,)), dma((3,)),
            dma((2, 3)), dma((2, 3)), dma((2, 2)), dma((2, 2)), dma((2,)), dma((2,)),
            dma(()), dma(()), dma((3,)), dma((3,)), dma((3,)), dma((3,)), dma(()), dma(()), dma(()), dma(()),
            dma((7,)), dma((7,)),
            dma((2, 2)), dma((2, 2)), dma((2,)), dma((2,)),
            dma((12,)), dma((12,)),
        ],
        compiler_params=pltpu.CompilerParams(
            collective_id=0, has_side_effects=True, vmem_limit_bytes=44 * 1024 * 1024
        ),
        name="exchange",
    )(tile_block, tile_block.reshape(1, -1), rhs_atlas.reshape(tiles), panels, diag_inverse)

    trailing, solved = pl.pallas_call(
        finish_body,
        out_shape=(jax.ShapeDtypeStruct(tiles, F32), jax.ShapeDtypeStruct((2, NB, W), F32)),
        in_specs=[smem, vmem, vmem, vmem],
        out_specs=(hbm, hbm),
        scratch_shapes=[pltpu.VMEM((4, NB, W), F32), dma((4,)), dma(())],
        compiler_params=pltpu.CompilerParams(vmem_limit_bytes=4 * 1024 * 1024),
        name="finish",
    )(placing, recv, upd, solved)
    return solved, trailing.reshape(TILES * NB, W)


def solution(mesh):
    placed = (P("row", "col"), P(), P(None, "col", "row"), P())
    return jax.shard_map(
        shards,
        mesh=mesh,
        in_specs=placed,
        out_specs=(P(None, None, "col"), P("row", "col")),
        check_vma=False,
    )
```

```python
import jax
import jax.numpy as jnp
from jax import lax
from jax.experimental import pallas as pl
from jax.experimental.pallas import tpu as pltpu
from jax.sharding import PartitionSpec as P

MESH = pl.DeviceIdType.MESH
F32 = jnp.float32
BF16 = jnp.bfloat16
NB = 512
W = 256
ROWS = 8
TILES = 16
Q = 4
HB = 2 * NB


def split(v):
    hi = v.astype(BF16)
    return hi, (v - hi.astype(F32)).astype(BF16)


def dot_t(a, b):
    return lax.dot_general(
        a, b, (((0,), (0,)), ((), ())), precision=lax.Precision.HIGHEST, preferred_element_type=F32
    )


def exchange(
    tb, tbv, rhs, panels, dinv,
    recv, upd, solved, placing,
    rhs_v, send_v, lg, sg, sh, sl, lh, ll, mm, xb, rs, rr, b1, dv, first_n, order,
    loc, b1z_s, b1z_r, b1g_s, b1g_r, b1o_s, b1o_r, lg_s, lg_r, lo_s, lo_r, lf_s, lf_r,
    mx_s, mx_r, rs_s, rs_r, ag_s, ag_r, rx_s, rx_r, hx_s, hx_r, az_s, az_r,
    sg_s, sg_r, sf_s, sf_r, u_s, u_r,
):
    row = lax.axis_index("row")
    col = lax.axis_index("col")
    z, core = row // 2, row % 2
    x, y = col // Q, col % Q
    g = x + core * (y - x)
    o = y + core * (x - y)
    left_g, right_g, far_g = (g + 3) % Q, (g + 1) % Q, (g + 2) % Q
    left_o, right_o, far_o = (o + 3) % Q, (o + 1) % Q, (o + 2) % Q

    def col_of(gg, oo):
        return gg * Q + oo + core * ((oo * Q + gg) - (gg * Q + oo))

    def at_g(d):
        return (row, col_of((g + d) % Q, o))

    def at_o(d):
        return (row, col_of(g, (o + d) % Q))

    def at_z(d):
        return (((z + d) % Q) * 2 + core, col)

    def at_row(d):
        return ((row + d) % ROWS, col)

    sibling = (z * 2 + 1 - core, col)

    def remote(src, dst, ss, rsem, dev):
        return pltpu.make_async_remote_copy(
            src_ref=src, dst_ref=dst, send_sem=ss, recv_sem=rsem, device_id=dev, device_id_type=MESH
        )

    def landed(ref, ss, rsem, dev):
        remote(ref, ref, ss, rsem, dev).wait_recv()

    sent = []

    def send(src, dst, ss, rsem, dev):
        c = remote(src, dst, ss, rsem, dev)
        c.start()
        sent.append(c)

    rhs_in = pltpu.make_async_copy(rhs, rhs_v, loc.at[0])
    rhs_in.start()

    def eighth(h, p, gg):
        return panels.at[p, :, pl.ds(pl.multiple_of(gg * (Q * NB) + h * HB, HB), HB)]

    own_l = []
    for h in range(2):
        for p in range(2):
            c = pltpu.make_async_copy(eighth(h, p, g), lg.at[h, p, o, g], loc.at[6 + 2 * h + p])
            c.start()
            own_l.append(c)
    dinv_in = pltpu.make_async_copy(dinv, dv, loc.at[3])
    dinv_in.start()

    barrier = pltpu.get_barrier_semaphore()
    for d in range(1, ROWS):
        pl.semaphore_signal(barrier, inc=1, device_id=at_row(d), device_id_type=MESH)
    for d in range(1, Q):
        pl.semaphore_signal(barrier, inc=1, device_id=at_g(d), device_id_type=MESH)
        pl.semaphore_signal(barrier, inc=1, device_id=at_o(d), device_id_type=MESH)

    mine = [tb[row * TILES + t] for t in range(TILES)]
    goal = [v % ROWS for v in mine]
    for r in range(ROWS):
        low, high = jnp.int32(0), jnp.int32(0)
        for t in range(TILES):
            high = jnp.where(goal[t] == r, t, high)
            low = jnp.where(goal[TILES - 1 - t] == r, TILES - 1 - t, low)
        order[2 * r] = low
        order[2 * r + 1] = high
    for p in range(2):
        where_p, held = jnp.int32(0), jnp.int32(0)
        for t in range(TILES):
            where_p = jnp.where(mine[t] == p, t, where_p)
            held = jnp.where(mine[t] == p, 1, held)
        order[TILES + 2 * p] = where_p
        order[TILES + 2 * p + 1] = held

    pl.semaphore_wait(barrier, ROWS - 1 + 2 * (Q - 1))

    def head(c2):
        return panels.at[0, :, pl.ds(pl.multiple_of(c2 * W, W), W)]

    @pl.when(row == 1)
    def _():
        for d in range(1, ROWS):
            r2 = (row + d) % ROWS
            c2 = r2 % 2
            g2 = x + c2 * (y - x)
            o2 = y + c2 * (x - y)
            remote(head(c2), b1.at[o2, g2], b1z_s.at[d - 1], b1z_r, (r2, col)).start()
        own = pltpu.make_async_copy(head(core), b1.at[o, g], loc.at[4])
        own.start()
        own.wait()

    def scatter(h):
        for p in range(2):
            for d in (2, 1, 3):
                send(
                    eighth(h, p, (g + d) % Q), lg.at[h, p, o, g],
                    lg_s.at[h, p, d - 1], lg_r.at[h, p, d - 1], at_g(d),
                )

    scatter(0)

    rhs_in.wait()
    for p in range(2):
        mm[p] = rhs_v[order[TILES + 2 * p]] * order[TILES + 2 * p + 1].astype(F32)
    half = pl.ds(pl.multiple_of(core * W, W), W)
    other = pl.ds(pl.multiple_of((1 - core) * W, W), W)
    send(mm.at[:, other], xb, mx_s, mx_r, sibling)

    def reorder(t, carry):
        send_v[t] = rhs_v[order[t]]
        return carry

    lax.fori_loop(0, TILES, reorder, 0)

    @pl.when(row != 1)
    def _():
        landed(b1.at[o, g], b1z_s.at[0], b1z_r, (1, col))

    for d in range(1, Q):
        send(b1.at[o, g], b1.at[o, g], b1g_s.at[d - 1], b1g_r.at[d - 1], at_g(d))
    swap = sent.pop(-4)
    scatter(1)

    swap.wait_send()
    landed(xb, mx_s, mx_r, sibling)
    mm[:, half] = mm[:, half] + xb[...]

    def piece(zz):
        return pl.ds(pl.multiple_of(core * W + zz * (W // Q), W // Q), W // Q)

    for d in (2, 1, 3):
        send(mm.at[:, piece((z + d) % Q)], rs.at[d - 1], rs_s.at[d - 1], rs_r.at[d - 1], at_z(d))
    pieces = [sent.pop() for _ in range(Q - 1)]

    for d in range(1, Q):
        landed(rs.at[d - 1], rs_s.at[d - 1], rs_r.at[d - 1], at_z(d))
    rr[:, piece(z)] = mm[:, piece(z)] + (rs[0] + rs[1] + rs[2])
    for d in (2, 1, 3):
        send(rr.at[:, piece(z)], rr.at[:, piece(z)], ag_s.at[d - 1], ag_r.at[d - 1], at_z(d))

    def gathered(h):
        for p in range(2):
            own_l[2 * h + p].wait()
            for d in range(1, Q):
                landed(lg.at[h, p, o, (g + Q - d) % Q], lg_s.at[h, p, d - 1], lg_r.at[h, p, d - 1], at_g(d))

    def first_leg(h):
        for p in range(2):
            for n, d in ((p, (1, Q - 1)[p]), (1 - p, (Q - 1, 1)[p])):
                send(lg.at[h, p, o], lg.at[h, p, o], lo_s.at[h, p, n], lo_r.at[h, p, n], at_o(d))

    def second_leg(h):
        for p in range(2):
            d = (1, Q - 1)[p]
            oo = (left_o, right_o)[p]
            landed(lg.at[h, p, oo], lo_s.at[h, p, p], lo_r.at[h, p, p], at_o(d))
            send(lg.at[h, p, oo], lg.at[h, p, oo], lf_s.at[h, p], lf_r.at[h, p], at_o(d))

    def all_legs(h):
        for p in range(2):
            d = (Q - 1, 1)[p]
            oo = (right_o, left_o)[p]
            landed(lg.at[h, p, oo], lo_s.at[h, p, 1 - p], lo_r.at[h, p, 1 - p], at_o(d))
            landed(lg.at[h, p, far_o], lf_s.at[h, p], lf_r.at[h, p], at_o(1))

    for d in range(1, Q):
        landed(b1.at[o, (g + Q - d) % Q], b1g_s.at[d - 1], b1g_r.at[d - 1], at_g(d))
    for d in range(1, Q):
        send(b1.at[o], b1.at[o], b1o_s.at[d - 1], b1o_r.at[d - 1], at_o(d))
    gathered(0)
    first_leg(0)
    gathered(1)

    for d in range(1, Q):
        landed(rr.at[:, piece((z + Q - d) % Q)], ag_s.at[d - 1], ag_r.at[d - 1], at_z(d))
    send(rr.at[:, half], rr.at[:, half], rx_s, rx_r, sibling)

    for d in (4, 2, 6, 3, 5, 1, 7):
        send(
            send_v.at[pl.ds(2 * ((row + d) % ROWS), 2)], recv.at[pl.ds(2 * row, 2)],
            az_s.at[d - 1], az_r.at[d - 1], at_row(d),
        )
    own_t = pltpu.make_async_copy(send_v.at[pl.ds(2 * row, 2)], recv.at[pl.ds(2 * row, 2)], loc.at[5])
    own_t.start()
    dinv_in.wait()
    landed(rr.at[:, other], rx_s, rx_r, sibling)

    def arrange(which, value):
        first_n[...] = value
        solved[which] = value

        def put(n, carry):
            oo, gg = n // Q, n % Q
            sg[g, which, pl.ds(pl.multiple_of(n * 32, 32), 32)] = first_n[
                pl.ds(pl.multiple_of(col_of(gg, oo) * 32, 32), 32)
            ]
            return carry

        lax.fori_loop(0, TILES, put, 0)

    def spread(p):
        for n, d in ((p, (1, Q - 1)[p]), (1 - p, (Q - 1, 1)[p])):
            send(sg.at[g, p], sg.at[g, p], sg_s.at[p, n], sg_r.at[p, n], at_g(d))

    def solve(which, block):
        return jnp.dot(dv[which], block, precision=lax.Precision.HIGHEST, preferred_element_type=F32)

    arrange(0, solve(0, rr[0]))
    spread(0)
    for d in range(1, Q):
        landed(b1.at[(o + Q - d) % Q], b1o_s.at[d - 1], b1o_r.at[d - 1], at_o(d))
    for c in pieces:
        c.wait_send()
    mm[0, half] = rr[1, half] - dot_t(b1[...].reshape(NB, W), sg[g, 0])
    send(mm.at[0, half], mm.at[0, half], hx_s, hx_r, sibling)
    landed(mm.at[0, other], hx_s, hx_r, sibling)
    arrange(1, solve(1, mm[0]))
    spread(1)
    second_leg(0)
    first_leg(1)

    def split_solved(gg, p):
        hi, lo = split(sg[gg, p])
        sh[gg, pl.ds(p * NB, NB)] = hi
        sl[gg, pl.ds(p * NB, NB)] = lo

    for p in range(2):
        d = (1, Q - 1)[p]
        gg = (left_g, right_g)[p]
        landed(sg.at[gg, p], sg_s.at[p, p], sg_r.at[p, p], at_g(d))
        send(sg.at[gg, p], sg.at[gg, p], sf_s.at[p], sf_r.at[p], at_g(d))
        split_solved(g, p)
        split_solved(gg, p)
    second_leg(1)
    for p in range(2):
        d = (Q - 1, 1)[p]
        gg = (right_g, left_g)[p]
        landed(sg.at[gg, p], sg_s.at[p, 1 - p], sg_r.at[p, 1 - p], at_g(d))
        split_solved(gg, p)
    for p in range(2):
        landed(sg.at[far_g, p], sf_s.at[p], sf_r.at[p], at_g(1))
        split_solved(far_g, p)

    def tile_step(i, carry):
        def turn(n, inner):
            p = n // Q
            keep = jnp.where((i == 0) & (g == 0) & (row <= p), 0.0, 1.0).astype(F32)
            part = lg[i // 2, p, n % Q, :, :, pl.ds(pl.multiple_of((i % 2) * NB, NB), NB)].reshape(4 * 32, NB)
            hi, lo = split(part.T * keep)
            at = pl.ds(pl.multiple_of(n * 128, 128), 128)
            lh[:, at] = hi
            ll[:, at] = lo
            return inner

        lax.fori_loop(0, 2 * Q, turn, 0)

        def dest_step(m, inner):
            d = (m + 2) % Q
            gg = (g + d) % Q
            a, b = lh[...], sh[gg]
            acc = jnp.dot(a, b, preferred_element_type=F32)
            acc += jnp.dot(a, sl[gg], preferred_element_type=F32)
            acc += jnp.dot(ll[...], b, preferred_element_type=F32)

            @pl.when(d != 0)
            def _():
                n = Q * d - Q + i
                rhs_v[n] = acc
                remote(rhs_v.at[n], upd.at[Q * g + i], u_s.at[n], u_r.at[n], (row, col_of(gg, o))).start()

            @pl.when(d == 0)
            def _():
                upd[Q * g + i] = acc

            return inner

        lax.fori_loop(0, Q, dest_step, 0)
        return carry

    all_legs(0)
    lax.fori_loop(0, 2, tile_step, 0)
    all_legs(1)
    lax.fori_loop(2, Q, tile_step, 0)

    ids = tbv[...]
    every = lax.broadcasted_iota(jnp.int32, (TILES, ROWS * TILES), 1)
    want = lax.broadcasted_iota(jnp.int32, (TILES, ROWS * TILES), 0) * ROWS + row
    where_is = jnp.sum(jnp.where(ids == want, every, 0), axis=1, keepdims=True)
    before = (every < where_is) & (ids % ROWS == row)
    count = jnp.sum(before.astype(jnp.int32), axis=1, keepdims=True)
    count = jnp.broadcast_to(count, (TILES, ROWS * TILES))
    placing[...] = count

    own_t.wait()
    for d in range(1, ROWS):
        landed(recv.at[pl.ds(2 * ((row + ROWS - d) % ROWS), 2)], az_s.at[d - 1], az_r.at[d - 1], at_row(d))
    for c in sent:
        c.wait_send()

    @pl.when(row == 1)
    def _():
        for d in range(1, ROWS):
            r2 = (row + d) % ROWS
            remote(head(r2 % 2), b1.at[o, g], b1z_s.at[d - 1], b1z_r, (r2, col)).wait_send()

    for i in range(Q):
        for d in range(1, Q):
            n = Q * d - Q + i
            remote(rhs_v.at[n], upd.at[Q * g + i], u_s.at[n], u_r.at[n], at_g(d)).wait_send()
            landed(upd.at[Q * ((g + Q - d) % Q) + i], u_s.at[n], u_r.at[n], at_g(d))


def finish_body(placing, recv, upd, solved, out, solved_out, stage, sems, sol_sem):
    sol = pltpu.make_async_copy(solved, solved_out, sol_sem)
    sol.start()
    depth = stage.shape[0]

    def put(b):
        return pltpu.make_async_copy(stage.at[b % depth], out.at[b], sems.at[b % depth])

    for b in range(TILES):
        if b >= depth:
            put(b - depth).wait()
        stage[b % depth] = recv[placing[b, 0]] - upd[b]
        put(b).start()
    for b in range(TILES - depth, TILES):
        put(b).wait()
    sol.wait()


def shards(rhs_atlas, tile_block, panels, diag_inverse):
    dma = pltpu.SemaphoreType.DMA
    hbm = pl.BlockSpec(memory_space=pltpu.HBM)
    vmem = pl.BlockSpec(memory_space=pltpu.VMEM)
    smem = pl.BlockSpec(memory_space=pltpu.SMEM)
    tiles = (TILES, NB, W)
    recv, upd, solved, placing = pl.pallas_call(
        exchange,
        out_shape=(
            pltpu.VMEM(tiles, F32),
            pltpu.VMEM(tiles, F32),
            pltpu.VMEM((2, NB, W), F32),
            pltpu.VMEM((TILES, ROWS * TILES), jnp.int32),
        ),
        in_specs=[smem, vmem, hbm, hbm, hbm],
        out_specs=(vmem, vmem, vmem, vmem),
        scratch_shapes=[
            pltpu.VMEM(tiles, F32),
            pltpu.VMEM(tiles, F32),
            pltpu.VMEM((2, 2, Q, Q, 32, HB), F32),
            pltpu.VMEM((Q, 2, NB, W), F32),
            pltpu.VMEM((Q, 2 * NB, W), BF16),
            pltpu.VMEM((Q, 2 * NB, W), BF16),
            pltpu.VMEM((NB, 2 * NB), BF16),
            pltpu.VMEM((NB, 2 * NB), BF16),
            pltpu.VMEM((2, NB, W), F32),
            pltpu.VMEM((2, W, W), F32),
            pltpu.VMEM((Q - 1, 2, W // Q, W), F32),
            pltpu.VMEM((2, NB, W), F32),
            pltpu.VMEM((Q, Q, 32, W), F32),
            pltpu.VMEM((2, NB, NB), F32),
            pltpu.VMEM((NB, W), F32),
            pltpu.SMEM((TILES + 4,), jnp.int32),
            dma((10,)),
            dma((7,)), dma(()), dma((3,)), dma((3,)), dma((3,)), dma((3,)),
            dma((2, 2, 3)), dma((2, 2, 3)), dma((2, 2, 2)), dma((2, 2, 2)), dma((2, 2)), dma((2, 2)),
            dma(()), dma(()), dma((3,)), dma((3,)), dma((3,)), dma((3,)), dma(()), dma(()), dma(()), dma(()),
            dma((7,)), dma((7,)),
            dma((2, 2)), dma((2, 2)), dma((2,)), dma((2,)),
            dma((12,)), dma((12,)),
        ],
        compiler_params=pltpu.CompilerParams(
            collective_id=0, has_side_effects=True, vmem_limit_bytes=44 * 1024 * 1024
        ),
        name="exchange",
    )(tile_block, tile_block.reshape(1, -1), rhs_atlas.reshape(tiles), panels, diag_inverse)

    trailing, solved = pl.pallas_call(
        finish_body,
        out_shape=(jax.ShapeDtypeStruct(tiles, F32), jax.ShapeDtypeStruct((2, NB, W), F32)),
        in_specs=[vmem, vmem, vmem, vmem],
        out_specs=(hbm, hbm),
        scratch_shapes=[pltpu.VMEM((8, NB, W), F32), dma((8,)), dma(())],
        compiler_params=pltpu.CompilerParams(vmem_limit_bytes=6 * 1024 * 1024),
        name="finish",
    )(placing, recv, upd, solved)
    return solved, trailing.reshape(TILES * NB, W)


def solution(mesh):
    placed = (P("row", "col"), P(), P(None, "col", "row"), P())
    return jax.shard_map(
        shards,
        mesh=mesh,
        in_specs=placed,
        out_specs=(P(None, None, "col"), P("row", "col")),
        check_vma=False,
    )
```

```python
import jax
import jax.numpy as jnp
from jax import lax
from jax.experimental import pallas as pl
from jax.experimental.pallas import tpu as pltpu
from jax.sharding import PartitionSpec as P

MESH = pl.DeviceIdType.MESH
F32 = jnp.float32
BF16 = jnp.bfloat16
NB = 512
W = 256
ROWS = 8
TILES = 16
Q = 4
HB = 2 * NB


def split(v):
    hi = v.astype(BF16)
    return hi, (v - hi.astype(F32)).astype(BF16)


def dot_t(a, b):
    return lax.dot_general(
        a, b, (((0,), (0,)), ((), ())), precision=lax.Precision.HIGHEST, preferred_element_type=F32
    )


def exchange(
    tb_hbm, tbv_hbm, rhs, panels, dinv,
    recv, upd, solved, placing,
    rhs_v, send_v, lg, sg, sh, sl, lh, ll, mm, xb, rs, rr, b1, dv, first_n, tb, tbv, order,
    loc, b1z_s, b1z_r, b1g_s, b1g_r, b1o_s, b1o_r, lg_s, lg_r, lo_s, lo_r,
    mx_s, mx_r, rs_s, rs_r, ag_s, ag_r, rx_s, rx_r, hx_s, hx_r, az_s, az_r,
    sg_s, sg_r, u_s, u_r,
):
    row = lax.axis_index("row")
    col = lax.axis_index("col")
    z, core = row // 2, row % 2
    x, y = col // Q, col % Q
    g = x + core * (y - x)
    o = y + core * (x - y)
    left_g, right_g, far_g = (g + 3) % Q, (g + 1) % Q, (g + 2) % Q
    left_o, right_o, far_o = (o + 3) % Q, (o + 1) % Q, (o + 2) % Q

    def col_of(gg, oo):
        return gg * Q + oo + core * ((oo * Q + gg) - (gg * Q + oo))

    def at_g(d):
        return (row, col_of((g + d) % Q, o))

    def at_o(d):
        return (row, col_of(g, (o + d) % Q))

    def at_z(d):
        return (((z + d) % Q) * 2 + core, col)

    def at_row(d):
        return ((row + d) % ROWS, col)

    sibling = (z * 2 + 1 - core, col)

    def remote(src, dst, ss, rsem, dev):
        return pltpu.make_async_remote_copy(
            src_ref=src, dst_ref=dst, send_sem=ss, recv_sem=rsem, device_id=dev, device_id_type=MESH
        )

    def landed(ref, ss, rsem, dev):
        remote(ref, ref, ss, rsem, dev).wait_recv()

    def send(src, dst, ss, rsem, dev):
        remote(src, dst, ss, rsem, dev).start()

    def left_here(ref, ss):
        remote(ref, ref, ss, ss, sibling).wait_send()

    def eighth(h, gg):
        return panels.at[:, :, pl.ds(pl.multiple_of(gg * (Q * NB) + h * HB, HB), HB)]

    barrier = pltpu.get_barrier_semaphore()
    for d in range(1, ROWS):
        pl.semaphore_signal(barrier, inc=1, device_id=at_row(d), device_id_type=MESH)
    for d in range(1, Q):
        pl.semaphore_signal(barrier, inc=1, device_id=at_g(d), device_id_type=MESH)
        pl.semaphore_signal(barrier, inc=1, device_id=at_o(d), device_id_type=MESH)

    tb_in = pltpu.make_async_copy(tb_hbm, tb, loc.at[4])
    tb_in.start()
    rhs_in = pltpu.make_async_copy(rhs, rhs_v, loc.at[0])
    rhs_in.start()
    own_l = [pltpu.make_async_copy(eighth(h, g), lg.at[h, :, o, g], loc.at[1 + h]) for h in range(2)]
    for c in own_l:
        c.start()
    dinv_in = pltpu.make_async_copy(dinv, dv, loc.at[3])
    dinv_in.start()
    tb_in.wait()

    mine = [tb[row * TILES + t] for t in range(TILES)]
    goal = [v % ROWS for v in mine]
    for r in range(ROWS):
        low, high = jnp.int32(0), jnp.int32(0)
        for t in range(TILES):
            high = jnp.where(goal[t] == r, t, high)
            low = jnp.where(goal[TILES - 1 - t] == r, TILES - 1 - t, low)
        order[2 * r] = low
        order[2 * r + 1] = high
    for p in range(2):
        where_p, held = jnp.int32(0), jnp.int32(0)
        for t in range(TILES):
            where_p = jnp.where(mine[t] == p, t, where_p)
            held = jnp.where(mine[t] == p, 1, held)
        order[TILES + 2 * p] = where_p
        order[TILES + 2 * p + 1] = held

    pl.semaphore_wait(barrier, ROWS - 1 + 2 * (Q - 1))

    def head(c2):
        return panels.at[0, :, pl.ds(pl.multiple_of(c2 * W, W), W)]

    @pl.when(row == 1)
    def _():
        for d in range(1, ROWS):
            r2 = (row + d) % ROWS
            c2 = r2 % 2
            g2 = x + c2 * (y - x)
            o2 = y + c2 * (x - y)
            send(head(c2), b1.at[o2, g2], b1z_s, b1z_r, (r2, col))
        own = pltpu.make_async_copy(head(core), b1.at[o, g], loc.at[4])
        own.start()
        own.wait()

    def scatter(h):
        for d in (2, 1, 3):
            send(eighth(h, (g + d) % Q), lg.at[h, :, o, g], lg_s, lg_r.at[h], at_g(d))

    scatter(0)

    rhs_in.wait()
    for p in range(2):
        mm[p] = rhs_v[order[TILES + 2 * p]] * order[TILES + 2 * p + 1].astype(F32)
    half = pl.ds(pl.multiple_of(core * W, W), W)
    other = pl.ds(pl.multiple_of((1 - core) * W, W), W)
    send(mm.at[:, other], xb, mx_s, mx_r, sibling)

    def reorder(t, carry):
        send_v[t] = rhs_v[order[t]]
        return carry

    lax.fori_loop(0, TILES, reorder, 0)

    @pl.when(row != 1)
    def _():
        landed(b1.at[o, g], b1z_s, b1z_r, (1, col))

    for d in range(1, Q):
        send(b1.at[o, g], b1.at[o, g], b1g_s, b1g_r, at_g(d))
    scatter(1)

    left_here(mm.at[:, other], mx_s)
    landed(xb, mx_s, mx_r, sibling)
    mm[:, half] = mm[:, half] + xb[...]

    def piece(zz):
        return pl.ds(pl.multiple_of(core * W + zz * (W // Q), W // Q), W // Q)

    for d in (2, 1, 3):
        send(mm.at[:, piece((z + d) % Q)], rs.at[d - 1], rs_s, rs_r, at_z(d))
    landed(rs, rs_s, rs_r, at_z(1))
    rr[:, piece(z)] = mm[:, piece(z)] + (rs[0] + rs[1] + rs[2])
    for d in (2, 1, 3):
        send(rr.at[:, piece(z)], rr.at[:, piece(z)], ag_s, ag_r, at_z(d))

    def gathered(h):
        own_l[h].wait()
        landed(lg.at[h, :, o, pl.ds(0, Q - 1)], lg_s, lg_r.at[h], at_g(1))

    def legs(p):
        return ((1, 0), (Q - 1, 2)) if p == 0 else ((Q - 1, 1), (1, 2))

    def first_leg(h):
        for p in range(2):
            for d, n in legs(p):
                send(lg.at[h, p, o], lg.at[h, p, o], lo_s, lo_r.at[h, n], at_o(d))

    def second_leg(h):
        for p in range(2):
            d = (1, Q - 1)[p]
            oo = (left_o, right_o)[p]
            landed(lg.at[h, p, oo], lo_s, lo_r.at[h, p], at_o(d))
            send(lg.at[h, p, oo], lg.at[h, p, oo], lo_s, lo_r.at[h, 2], at_o(d))

    def all_legs(h):
        landed(lg.at[h, 0], lo_s, lo_r.at[h, 2], at_o(1))

    landed(b1.at[o, pl.ds(0, Q - 1)], b1g_s, b1g_r, at_g(1))
    for d in (2, 1, 3):
        send(b1.at[o], b1.at[o], b1o_s, b1o_r, at_o(d))
    gathered(0)
    first_leg(0)
    gathered(1)

    landed(rs, ag_s, ag_r, at_z(1))
    send(rr.at[:, half], rr.at[:, half], rx_s, rx_r, sibling)

    for d in (4, 2, 6, 3, 5, 1, 7):
        send(send_v.at[pl.ds(2 * ((row + d) % ROWS), 2)], recv.at[pl.ds(2 * row, 2)], az_s, az_r, at_row(d))
    own_t = pltpu.make_async_copy(send_v.at[pl.ds(2 * row, 2)], recv.at[pl.ds(2 * row, 2)], loc.at[4])
    own_t.start()
    dinv_in.wait()
    landed(rr.at[:, other], rx_s, rx_r, sibling)

    def arrange(which, value):
        first_n[...] = value
        solved[which] = value

        def put(n, carry):
            oo, gg = n // Q, n % Q
            sg[g, which, pl.ds(pl.multiple_of(n * 32, 32), 32)] = first_n[
                pl.ds(pl.multiple_of(col_of(gg, oo) * 32, 32), 32)
            ]
            return carry

        lax.fori_loop(0, TILES, put, 0)

    def spread(p):
        for d, n in legs(p):
            send(sg.at[g, p], sg.at[g, p], sg_s, sg_r.at[n], at_g(d))

    def solve(which, block):
        return jnp.dot(dv[which], block, precision=lax.Precision.HIGHEST, preferred_element_type=F32)

    arrange(0, solve(0, rr[0]))
    spread(0)
    landed(b1.at[pl.ds(0, Q - 1)], b1o_s, b1o_r, at_o(1))
    left_here(rs, rs_s)
    mm[0, half] = rr[1, half] - dot_t(b1[...].reshape(NB, W), sg[g, 0])
    send(mm.at[0, half], mm.at[0, half], hx_s, hx_r, sibling)
    landed(mm.at[0, other], hx_s, hx_r, sibling)
    arrange(1, solve(1, mm[0]))
    spread(1)
    second_leg(0)
    first_leg(1)

    def split_solved(gg, p):
        hi, lo = split(sg[gg, p])
        sh[gg, pl.ds(p * NB, NB)] = hi
        sl[gg, pl.ds(p * NB, NB)] = lo

    for p in range(2):
        d = (1, Q - 1)[p]
        gg = (left_g, right_g)[p]
        landed(sg.at[gg, p], sg_s, sg_r.at[p], at_g(d))
        send(sg.at[gg, p], sg.at[gg, p], sg_s, sg_r.at[2], at_g(d))
        split_solved(g, p)
        split_solved(gg, p)
    second_leg(1)
    landed(sg.at[pl.ds(0, 2)], sg_s, sg_r.at[2], at_g(1))
    for p in range(2):
        split_solved((right_g, left_g)[p], p)
        split_solved(far_g, p)

    def tile_step(i, carry):
        def turn(n, inner):
            p = n // Q
            keep = jnp.where((i == 0) & (g == 0) & (row <= p), 0.0, 1.0).astype(F32)
            part = lg[i // 2, p, n % Q, :, :, pl.ds(pl.multiple_of((i % 2) * NB, NB), NB)].reshape(4 * 32, NB)
            hi, lo = split(part.T * keep)
            at = pl.ds(pl.multiple_of(n * 128, 128), 128)
            lh[:, at] = hi
            ll[:, at] = lo
            return inner

        lax.fori_loop(0, 2 * Q, turn, 0)

        def dest_step(m, inner):
            d = (m + 2) % Q
            gg = (g + d) % Q
            a, b = lh[...], sh[gg]
            acc = jnp.dot(a, b, preferred_element_type=F32)
            acc += jnp.dot(a, sl[gg], preferred_element_type=F32)
            acc += jnp.dot(ll[...], b, preferred_element_type=F32)

            @pl.when(d != 0)
            def _():
                n = Q * d - Q + i
                rhs_v[n] = acc
                send(rhs_v.at[n], upd.at[Q * g + i], u_s, u_r, (row, col_of(gg, o)))

            @pl.when(d == 0)
            def _():
                upd[Q * g + i] = acc

            return inner

        lax.fori_loop(0, Q, dest_step, 0)
        return carry

    tbv_in = pltpu.make_async_copy(tbv_hbm, tbv, loc.at[0])
    tbv_in.start()
    all_legs(0)
    lax.fori_loop(0, 2, tile_step, 0)
    all_legs(1)
    lax.fori_loop(2, Q, tile_step, 0)

    tbv_in.wait()
    ids = tbv[...]
    every = lax.broadcasted_iota(jnp.int32, (TILES, ROWS * TILES), 1)
    want = lax.broadcasted_iota(jnp.int32, (TILES, ROWS * TILES), 0) * ROWS + row
    where_is = jnp.sum(jnp.where(ids == want, every, 0), axis=1, keepdims=True)
    before = (every < where_is) & (ids % ROWS == row)
    count = jnp.sum(before.astype(jnp.int32), axis=1, keepdims=True)
    count = jnp.broadcast_to(count, (TILES, ROWS * TILES))
    placing[...] = count

    own_t.wait()
    landed(send_v.at[pl.ds(0, TILES - 2)], az_s, az_r, sibling)
    left_here(send_v.at[pl.ds(0, TILES - 2)], az_s)
    left_here(lg.at[0, 0, pl.ds(0, Q - 1)], lg_s)
    left_here(rhs_v.at[pl.ds(0, 3 * Q)], lo_s)
    left_here(b1.at[0, pl.ds(0, Q - 1)], b1g_s)
    left_here(b1.at[pl.ds(0, Q - 1)], b1o_s)
    left_here(rs, ag_s)
    left_here(rr.at[:, half], rx_s)
    left_here(mm.at[0, half], hx_s)
    left_here(rhs_v.at[pl.ds(0, 6)], sg_s)

    @pl.when(row == 1)
    def _():
        left_here(send_v.at[0, pl.ds(0, 32 * (ROWS - 1))], b1z_s)

    left_here(rhs_v.at[pl.ds(0, 3 * Q)], u_s)
    landed(rhs_v.at[pl.ds(0, 3 * Q)], u_s, u_r, at_g(1))


def finish_body(placing, recv, upd, solved, out, solved_out, stage, sems, sol_sem):
    sol = pltpu.make_async_copy(solved, solved_out, sol_sem)
    sol.start()
    depth = stage.shape[0]

    def put(b):
        return pltpu.make_async_copy(stage.at[b % depth], out.at[b], sems.at[b % depth])

    for b in range(TILES):
        if b >= depth:
            put(b - depth).wait()
        stage[b % depth] = recv[placing[b, 0]] - upd[b]
        put(b).start()
    for b in range(TILES - depth, TILES):
        put(b).wait()
    sol.wait()


def shards(rhs_atlas, tile_block, panels, diag_inverse):
    dma = pltpu.SemaphoreType.DMA
    hbm = pl.BlockSpec(memory_space=pltpu.HBM)
    vmem = pl.BlockSpec(memory_space=pltpu.VMEM)
    tiles = (TILES, NB, W)
    recv, upd, solved, placing = pl.pallas_call(
        exchange,
        out_shape=(
            pltpu.VMEM(tiles, F32),
            pltpu.VMEM(tiles, F32),
            pltpu.VMEM((2, NB, W), F32),
            pltpu.VMEM((TILES, ROWS * TILES), jnp.int32),
        ),
        in_specs=[hbm] * 5,
        out_specs=(vmem, vmem, vmem, vmem),
        scratch_shapes=[
            pltpu.VMEM(tiles, F32),
            pltpu.VMEM(tiles, F32),
            pltpu.VMEM((2, 2, Q, Q, 32, HB), F32),
            pltpu.VMEM((Q, 2, NB, W), F32),
            pltpu.VMEM((Q, 2 * NB, W), BF16),
            pltpu.VMEM((Q, 2 * NB, W), BF16),
            pltpu.VMEM((NB, 2 * NB), BF16),
            pltpu.VMEM((NB, 2 * NB), BF16),
            pltpu.VMEM((2, NB, W), F32),
            pltpu.VMEM((2, W, W), F32),
            pltpu.VMEM((Q - 1, 2, W // Q, W), F32),
            pltpu.VMEM((2, NB, W), F32),
            pltpu.VMEM((Q, Q, 32, W), F32),
            pltpu.VMEM((2, NB, NB), F32),
            pltpu.VMEM((NB, W), F32),
            pltpu.SMEM((ROWS * TILES,), jnp.int32),
            pltpu.VMEM((1, ROWS * TILES), jnp.int32),
            pltpu.SMEM((TILES + 4,), jnp.int32),
            dma((5,)), dma(()), dma(()), dma(()), dma(()), dma(()), dma(()), dma(()), dma((2,)), dma(()), dma((2, 3)),
            dma(()), dma(()), dma(()), dma(()), dma(()), dma(()), dma(()), dma(()), dma(()), dma(()), dma(()), dma(()),
            dma(()), dma((3,)), dma(()), dma(()),
        ],
        compiler_params=pltpu.CompilerParams(
            collective_id=0, has_side_effects=True, vmem_limit_bytes=44 * 1024 * 1024
        ),
        name="exchange",
    )(tile_block, tile_block.reshape(1, -1), rhs_atlas.reshape(tiles), panels, diag_inverse)

    trailing, solved = pl.pallas_call(
        finish_body,
        out_shape=(jax.ShapeDtypeStruct(tiles, F32), jax.ShapeDtypeStruct((2, NB, W), F32)),
        in_specs=[vmem, vmem, vmem, vmem],
        out_specs=(hbm, hbm),
        scratch_shapes=[pltpu.VMEM((8, NB, W), F32), dma((8,)), dma(())],
        compiler_params=pltpu.CompilerParams(vmem_limit_bytes=6 * 1024 * 1024),
        name="finish",
    )(placing, recv, upd, solved)
    return solved, trailing.reshape(TILES * NB, W)


def solution(mesh):
    placed = (P("row", "col"), P(), P(None, "col", "row"), P())
    return jax.shard_map(
        shards,
        mesh=mesh,
        in_specs=placed,
        out_specs=(P(None, None, "col"), P("row", "col")),
        check_vma=False,
    )
```

```python
import jax
import jax.numpy as jnp
from jax import lax
from jax.experimental import pallas as pl
from jax.experimental.pallas import tpu as pltpu
from jax.sharding import PartitionSpec as P

MESH = pl.DeviceIdType.MESH
F32 = jnp.float32
BF16 = jnp.bfloat16
NB = 512
W = 256
ROWS = 8
TILES = 16
Q = 4
HB = 2 * NB


def split(v):
    hi = v.astype(BF16)
    return hi, (v - hi.astype(F32)).astype(BF16)


def dot_t(a, b):
    return lax.dot_general(
        a, b, (((0,), (0,)), ((), ())), precision=lax.Precision.HIGHEST, preferred_element_type=F32
    )


def exchange(
    tb_hbm, tbv_hbm, rhs, panels, dinv,
    recv, upd, solved, placing,
    rhs_v, send_v, lg, sg, sh, sl, lh, ll, mm, xb, rs, rr, b1, dv, first_n, tb, tbv, order,
    loc, b1z_s, b1z_r, b1g_s, b1g_r, b1o_s, b1o_r, lg_s, lg_r, lo_s, lo_r,
    mx_s, mx_r, rs_s, rs_r, ag_s, ag_r, rx_s, rx_r, hx_s, hx_r, az_s, az_r,
    sg_s, sg_r, u_s, u_r,
):
    row = lax.axis_index("row")
    col = lax.axis_index("col")
    z, core = row // 2, row % 2
    x, y = col // Q, col % Q
    g = x + core * (y - x)
    o = y + core * (x - y)
    left_g, right_g, far_g = (g + 3) % Q, (g + 1) % Q, (g + 2) % Q
    left_o, right_o, far_o = (o + 3) % Q, (o + 1) % Q, (o + 2) % Q

    def col_of(gg, oo):
        return gg * Q + oo + core * ((oo * Q + gg) - (gg * Q + oo))

    def at_g(d):
        return (row, col_of((g + d) % Q, o))

    def at_o(d):
        return (row, col_of(g, (o + d) % Q))

    def at_z(d):
        return (((z + d) % Q) * 2 + core, col)

    def at_row(d):
        return ((row + d) % ROWS, col)

    sibling = (z * 2 + 1 - core, col)

    def remote(src, dst, ss, rsem, dev):
        return pltpu.make_async_remote_copy(
            src_ref=src, dst_ref=dst, send_sem=ss, recv_sem=rsem, device_id=dev, device_id_type=MESH
        )

    def landed(ref, ss, rsem, dev):
        remote(ref, ref, ss, rsem, dev).wait_recv()

    def send(src, dst, ss, rsem, dev):
        remote(src, dst, ss, rsem, dev).start()

    def left_here(ref, ss):
        remote(ref, ref, ss, ss, sibling).wait_send()

    def eighth(h, gg):
        return panels.at[:, :, pl.ds(pl.multiple_of(gg * (Q * NB) + h * HB, HB), HB)]

    barrier = pltpu.get_barrier_semaphore()
    for d in range(1, ROWS):
        pl.semaphore_signal(barrier, inc=1, device_id=at_row(d), device_id_type=MESH)
    for d in range(1, Q):
        pl.semaphore_signal(barrier, inc=1, device_id=at_g(d), device_id_type=MESH)
        pl.semaphore_signal(barrier, inc=1, device_id=at_o(d), device_id_type=MESH)

    tb_in = pltpu.make_async_copy(tb_hbm, tb, loc.at[4])
    tb_in.start()
    rhs_in = pltpu.make_async_copy(rhs, rhs_v, loc.at[0])
    rhs_in.start()
    own_l = [pltpu.make_async_copy(eighth(h, g), lg.at[h, :, o, g], loc.at[1 + h]) for h in range(2)]
    for c in own_l:
        c.start()
    dinv_in = pltpu.make_async_copy(dinv, dv, loc.at[3])
    dinv_in.start()
    tb_in.wait()

    mine = [tb[row * TILES + t] for t in range(TILES)]
    goal = [v % ROWS for v in mine]
    for r in range(ROWS):
        low, high = jnp.int32(0), jnp.int32(0)
        for t in range(TILES):
            high = jnp.where(goal[t] == r, t, high)
            low = jnp.where(goal[TILES - 1 - t] == r, TILES - 1 - t, low)
        order[2 * r] = low
        order[2 * r + 1] = high
    for p in range(2):
        where_p, held = jnp.int32(0), jnp.int32(0)
        for t in range(TILES):
            where_p = jnp.where(mine[t] == p, t, where_p)
            held = jnp.where(mine[t] == p, 1, held)
        order[TILES + 2 * p] = where_p
        order[TILES + 2 * p + 1] = held

    pl.semaphore_wait(barrier, ROWS - 1 + 2 * (Q - 1))

    def head(c2):
        return panels.at[0, :, pl.ds(pl.multiple_of(c2 * W, W), W)]

    @pl.when(row == 1)
    def _():
        for d in range(1, ROWS):
            r2 = (row + d) % ROWS
            c2 = r2 % 2
            g2 = x + c2 * (y - x)
            o2 = y + c2 * (x - y)
            send(head(c2), b1.at[o2, g2], b1z_s, b1z_r, (r2, col))
        own = pltpu.make_async_copy(head(core), b1.at[o, g], loc.at[4])
        own.start()
        own.wait()

    def scatter(h):
        for d in (2, 1, 3):
            send(eighth(h, (g + d) % Q), lg.at[h, :, o, g], lg_s, lg_r.at[h], at_g(d))

    scatter(0)

    rhs_in.wait()
    for p in range(2):
        mm[p] = rhs_v[order[TILES + 2 * p]] * order[TILES + 2 * p + 1].astype(F32)
    half = pl.ds(pl.multiple_of(core * W, W), W)
    other = pl.ds(pl.multiple_of((1 - core) * W, W), W)
    send(mm.at[:, other], xb, mx_s, mx_r, sibling)

    def reorder(t, carry):
        send_v[t] = rhs_v[order[t]]
        return carry

    lax.fori_loop(0, TILES, reorder, 0)

    @pl.when(row != 1)
    def _():
        landed(b1.at[o, g], b1z_s, b1z_r, (1, col))

    for d in range(1, Q):
        send(b1.at[o, g], b1.at[o, g], b1g_s, b1g_r, at_g(d))
    scatter(1)

    left_here(mm.at[:, other], mx_s)
    landed(xb, mx_s, mx_r, sibling)
    mm[:, half] = mm[:, half] + xb[...]

    def piece(zz):
        return pl.ds(pl.multiple_of(core * W + zz * (W // Q), W // Q), W // Q)

    for d in (2, 1, 3):
        send(mm.at[:, piece((z + d) % Q)], rs.at[d - 1], rs_s, rs_r, at_z(d))

    def gathered(h):
        own_l[h].wait()
        landed(lg.at[h, :, o, pl.ds(0, Q - 1)], lg_s, lg_r.at[h], at_g(1))

    def legs(p):
        return ((1, 0), (Q - 1, 2)) if p == 0 else ((Q - 1, 1), (1, 2))

    def first_leg(h):
        for p in range(2):
            for d, n in legs(p):
                send(lg.at[h, p, o], lg.at[h, p, o], lo_s, lo_r.at[h, n], at_o(d))

    def second_leg(h):
        for p in range(2):
            d = (1, Q - 1)[p]
            oo = (left_o, right_o)[p]
            landed(lg.at[h, p, oo], lo_s, lo_r.at[h, p], at_o(d))
            send(lg.at[h, p, oo], lg.at[h, p, oo], lo_s, lo_r.at[h, 2], at_o(d))

    def all_legs(h):
        landed(lg.at[h, 0], lo_s, lo_r.at[h, 2], at_o(1))

    landed(b1.at[o, pl.ds(0, Q - 1)], b1g_s, b1g_r, at_g(1))
    for d in (2, 1, 3):
        send(b1.at[o], b1.at[o], b1o_s, b1o_r, at_o(d))
    gathered(0)
    first_leg(0)

    landed(rs, rs_s, rs_r, at_z(1))
    rr[:, piece(z)] = mm[:, piece(z)] + (rs[0] + rs[1] + rs[2])
    for d in (2, 1, 3):
        send(rr.at[:, piece(z)], rr.at[:, piece(z)], ag_s, ag_r, at_z(d))

    gathered(1)

    landed(rs, ag_s, ag_r, at_z(1))
    send(rr.at[:, half], rr.at[:, half], rx_s, rx_r, sibling)

    for d in (4, 2, 6, 3, 5, 1, 7):
        send(send_v.at[pl.ds(2 * ((row + d) % ROWS), 2)], recv.at[pl.ds(2 * row, 2)], az_s, az_r, at_row(d))
    own_t = pltpu.make_async_copy(send_v.at[pl.ds(2 * row, 2)], recv.at[pl.ds(2 * row, 2)], loc.at[4])
    own_t.start()
    dinv_in.wait()
    landed(rr.at[:, other], rx_s, rx_r, sibling)

    def arrange(which, value):
        first_n[...] = value
        solved[which] = value

        def put(n, carry):
            oo, gg = n // Q, n % Q
            sg[g, which, pl.ds(pl.multiple_of(n * 32, 32), 32)] = first_n[
                pl.ds(pl.multiple_of(col_of(gg, oo) * 32, 32), 32)
            ]
            return carry

        lax.fori_loop(0, TILES, put, 0)

    def spread(p):
        for d, n in legs(p):
            send(sg.at[g, p], sg.at[g, p], sg_s, sg_r.at[n], at_g(d))

    def solve(which, block):
        return jnp.dot(dv[which], block, precision=lax.Precision.HIGHEST, preferred_element_type=F32)

    arrange(0, solve(0, rr[0]))
    spread(0)
    landed(b1.at[pl.ds(0, Q - 1)], b1o_s, b1o_r, at_o(1))
    left_here(rs, rs_s)
    mm[0, half] = rr[1, half] - dot_t(b1[...].reshape(NB, W), sg[g, 0])
    send(mm.at[0, half], mm.at[0, half], hx_s, hx_r, sibling)
    landed(mm.at[0, other], hx_s, hx_r, sibling)
    arrange(1, solve(1, mm[0]))
    spread(1)

    def split_solved(gg, p):
        hi, lo = split(sg[gg, p])
        sh[gg, pl.ds(p * NB, NB)] = hi
        sl[gg, pl.ds(p * NB, NB)] = lo

    def spread_on(p):
        d = (1, Q - 1)[p]
        gg = (left_g, right_g)[p]
        landed(sg.at[gg, p], sg_s, sg_r.at[p], at_g(d))
        send(sg.at[gg, p], sg.at[gg, p], sg_s, sg_r.at[2], at_g(d))

    spread_on(0)
    second_leg(0)
    spread_on(1)
    first_leg(1)
    for p in range(2):
        split_solved(g, p)
        split_solved((left_g, right_g)[p], p)
    landed(sg.at[pl.ds(0, 2)], sg_s, sg_r.at[2], at_g(1))
    for p in range(2):
        split_solved((right_g, left_g)[p], p)
        split_solved(far_g, p)

    def tile_step(i, carry):
        def turn(n, inner):
            p = n // Q
            keep = jnp.where((i == 0) & (g == 0) & (row <= p), 0.0, 1.0).astype(F32)
            part = lg[i // 2, p, n % Q, :, :, pl.ds(pl.multiple_of((i % 2) * NB, NB), NB)].reshape(4 * 32, NB)
            hi, lo = split(part.T * keep)
            at = pl.ds(pl.multiple_of(n * 128, 128), 128)
            lh[:, at] = hi
            ll[:, at] = lo
            return inner

        lax.fori_loop(0, 2 * Q, turn, 0)

        def dest_step(m, inner):
            d = (m + 2) % Q
            gg = (g + d) % Q
            a, b = lh[...], sh[gg]
            acc = jnp.dot(a, b, preferred_element_type=F32)
            acc += jnp.dot(a, sl[gg], preferred_element_type=F32)
            acc += jnp.dot(ll[...], b, preferred_element_type=F32)

            @pl.when(d != 0)
            def _():
                n = Q * d - Q + i
                rhs_v[n] = acc
                send(rhs_v.at[n], upd.at[Q * g + i], u_s, u_r, (row, col_of(gg, o)))

            @pl.when(d == 0)
            def _():
                upd[Q * g + i] = acc

            return inner

        lax.fori_loop(0, Q, dest_step, 0)
        return carry

    tbv_in = pltpu.make_async_copy(tbv_hbm, tbv, loc.at[0])
    tbv_in.start()
    all_legs(0)
    lax.fori_loop(0, 1, tile_step, 0)
    second_leg(1)
    lax.fori_loop(1, 2, tile_step, 0)
    all_legs(1)
    lax.fori_loop(2, Q, tile_step, 0)

    tbv_in.wait()
    ids = tbv[...]
    every = lax.broadcasted_iota(jnp.int32, (TILES, ROWS * TILES), 1)
    want = lax.broadcasted_iota(jnp.int32, (TILES, ROWS * TILES), 0) * ROWS + row
    where_is = jnp.sum(jnp.where(ids == want, every, 0), axis=1, keepdims=True)
    before = (every < where_is) & (ids % ROWS == row)
    count = jnp.sum(before.astype(jnp.int32), axis=1, keepdims=True)
    count = jnp.broadcast_to(count, (TILES, ROWS * TILES))
    placing[...] = count

    own_t.wait()
    landed(send_v.at[pl.ds(0, TILES - 2)], az_s, az_r, sibling)
    left_here(send_v.at[pl.ds(0, TILES - 2)], az_s)
    left_here(lg.at[0, 0, pl.ds(0, Q - 1)], lg_s)
    left_here(rhs_v.at[pl.ds(0, 3 * Q)], lo_s)
    left_here(b1.at[0, pl.ds(0, Q - 1)], b1g_s)
    left_here(b1.at[pl.ds(0, Q - 1)], b1o_s)
    left_here(rs, ag_s)
    left_here(rr.at[:, half], rx_s)
    left_here(mm.at[0, half], hx_s)
    left_here(rhs_v.at[pl.ds(0, 6)], sg_s)

    @pl.when(row == 1)
    def _():
        left_here(send_v.at[0, pl.ds(0, 32 * (ROWS - 1))], b1z_s)

    left_here(rhs_v.at[pl.ds(0, 3 * Q)], u_s)
    landed(rhs_v.at[pl.ds(0, 3 * Q)], u_s, u_r, at_g(1))


def finish_body(placing, recv, upd, solved, out, solved_out, stage, sems, sol_sem):
    sol = pltpu.make_async_copy(solved, solved_out, sol_sem)
    sol.start()
    depth = stage.shape[0]

    def put(b):
        return pltpu.make_async_copy(stage.at[b % depth], out.at[b], sems.at[b % depth])

    for b in range(TILES):
        if b >= depth:
            put(b - depth).wait()
        stage[b % depth] = recv[placing[b, 0]] - upd[b]
        put(b).start()
    for b in range(TILES - depth, TILES):
        put(b).wait()
    sol.wait()


def shards(rhs_atlas, tile_block, panels, diag_inverse):
    dma = pltpu.SemaphoreType.DMA
    hbm = pl.BlockSpec(memory_space=pltpu.HBM)
    vmem = pl.BlockSpec(memory_space=pltpu.VMEM)
    tiles = (TILES, NB, W)
    recv, upd, solved, placing = pl.pallas_call(
        exchange,
        out_shape=(
            pltpu.VMEM(tiles, F32),
            pltpu.VMEM(tiles, F32),
            pltpu.VMEM((2, NB, W), F32),
            pltpu.VMEM((TILES, ROWS * TILES), jnp.int32),
        ),
        in_specs=[hbm] * 5,
        out_specs=(vmem, vmem, vmem, vmem),
        scratch_shapes=[
            pltpu.VMEM(tiles, F32),
            pltpu.VMEM(tiles, F32),
            pltpu.VMEM((2, 2, Q, Q, 32, HB), F32),
            pltpu.VMEM((Q, 2, NB, W), F32),
            pltpu.VMEM((Q, 2 * NB, W), BF16),
            pltpu.VMEM((Q, 2 * NB, W), BF16),
            pltpu.VMEM((NB, 2 * NB), BF16),
            pltpu.VMEM((NB, 2 * NB), BF16),
            pltpu.VMEM((2, NB, W), F32),
            pltpu.VMEM((2, W, W), F32),
            pltpu.VMEM((Q - 1, 2, W // Q, W), F32),
            pltpu.VMEM((2, NB, W), F32),
            pltpu.VMEM((Q, Q, 32, W), F32),
            pltpu.VMEM((2, NB, NB), F32),
            pltpu.VMEM((NB, W), F32),
            pltpu.SMEM((ROWS * TILES,), jnp.int32),
            pltpu.VMEM((1, ROWS * TILES), jnp.int32),
            pltpu.SMEM((TILES + 4,), jnp.int32),
            dma((5,)), dma(()), dma(()), dma(()), dma(()), dma(()), dma(()), dma(()), dma((2,)), dma(()), dma((2, 3)),
            dma(()), dma(()), dma(()), dma(()), dma(()), dma(()), dma(()), dma(()), dma(()), dma(()), dma(()), dma(()),
            dma(()), dma((3,)), dma(()), dma(()),
        ],
        compiler_params=pltpu.CompilerParams(
            collective_id=0, has_side_effects=True, vmem_limit_bytes=44 * 1024 * 1024
        ),
        name="exchange",
    )(tile_block, tile_block.reshape(1, -1), rhs_atlas.reshape(tiles), panels, diag_inverse)

    trailing, solved = pl.pallas_call(
        finish_body,
        out_shape=(jax.ShapeDtypeStruct(tiles, F32), jax.ShapeDtypeStruct((2, NB, W), F32)),
        in_specs=[vmem, vmem, vmem, vmem],
        out_specs=(hbm, hbm),
        scratch_shapes=[pltpu.VMEM((8, NB, W), F32), dma((8,)), dma(())],
        compiler_params=pltpu.CompilerParams(vmem_limit_bytes=6 * 1024 * 1024),
        name="finish",
    )(placing, recv, upd, solved)
    return solved, trailing.reshape(TILES * NB, W)


def solution(mesh):
    placed = (P("row", "col"), P(), P(None, "col", "row"), P())
    return jax.shard_map(
        shards,
        mesh=mesh,
        in_specs=placed,
        out_specs=(P(None, None, "col"), P("row", "col")),
        check_vma=False,
    )
```

```python
import jax
import jax.numpy as jnp
from jax import lax
from jax.experimental import pallas as pl
from jax.experimental.pallas import tpu as pltpu
from jax.sharding import PartitionSpec as P

MESH = pl.DeviceIdType.MESH
F32 = jnp.float32
BF16 = jnp.bfloat16
NB = 512
W = 256
ROWS = 8
TILES = 16
Q = 4
HB = 2 * NB


def split(v):
    hi = v.astype(BF16)
    return hi, (v - hi.astype(F32)).astype(BF16)


def dot_t(a, b):
    return lax.dot_general(
        a, b, (((0,), (0,)), ((), ())), precision=lax.Precision.HIGHEST, preferred_element_type=F32
    )


def exchange(
    tb_hbm, tbv_hbm, rhs, panels, dinv,
    recv, upd, solved, placing,
    rhs_v, send_v, lg, sg, sh, sl, lh, ll, mm, xb, rs, rr, b1, dv, first_n, tb, tbv, order,
    loc, b1z_s, b1z_r, b1g_s, b1g_r, b1o_s, b1o_r, lg_s, lg_r, lo_s, lo_r,
    mx_s, mx_r, rs_s, rs_r, ag_s, ag_r, rx_s, rx_r, hx_s, hx_r, az_s, az_r,
    sg_s, sg_r, u_s, u_r,
):
    row = lax.axis_index("row")
    col = lax.axis_index("col")
    z, core = row // 2, row % 2
    x, y = col // Q, col % Q
    g = x + core * (y - x)
    o = y + core * (x - y)
    left_g, right_g, far_g = (g + 3) % Q, (g + 1) % Q, (g + 2) % Q
    left_o, right_o, far_o = (o + 3) % Q, (o + 1) % Q, (o + 2) % Q

    def col_of(gg, oo):
        return gg * Q + oo + core * ((oo * Q + gg) - (gg * Q + oo))

    def at_g(d):
        return (row, col_of((g + d) % Q, o))

    def at_o(d):
        return (row, col_of(g, (o + d) % Q))

    def at_z(d):
        return (((z + d) % Q) * 2 + core, col)

    def at_row(d):
        return ((row + d) % ROWS, col)

    sibling = (z * 2 + 1 - core, col)

    def remote(src, dst, ss, rsem, dev):
        return pltpu.make_async_remote_copy(
            src_ref=src, dst_ref=dst, send_sem=ss, recv_sem=rsem, device_id=dev, device_id_type=MESH
        )

    def landed(ref, ss, rsem, dev):
        remote(ref, ref, ss, rsem, dev).wait_recv()

    def send(src, dst, ss, rsem, dev):
        remote(src, dst, ss, rsem, dev).start()

    def left_here(ref, ss):
        remote(ref, ref, ss, ss, sibling).wait_send()

    def eighth(h, gg):
        return panels.at[:, :, pl.ds(pl.multiple_of(gg * (Q * NB) + h * HB, HB), HB)]

    barrier = pltpu.get_barrier_semaphore()
    for d in range(1, ROWS):
        pl.semaphore_signal(barrier, inc=1, device_id=at_row(d), device_id_type=MESH)
    for d in range(1, Q):
        pl.semaphore_signal(barrier, inc=1, device_id=at_g(d), device_id_type=MESH)
        pl.semaphore_signal(barrier, inc=1, device_id=at_o(d), device_id_type=MESH)

    tb_in = pltpu.make_async_copy(tb_hbm, tb, loc.at[4])
    tb_in.start()
    rhs_in = pltpu.make_async_copy(rhs, rhs_v, loc.at[0])
    rhs_in.start()
    own_l = [pltpu.make_async_copy(eighth(h, g), lg.at[h, :, o, g], loc.at[1 + h]) for h in range(2)]
    for c in own_l:
        c.start()
    dinv_in = pltpu.make_async_copy(dinv, dv, loc.at[3])
    dinv_in.start()
    tb_in.wait()

    mine = [tb[row * TILES + t] for t in range(TILES)]
    goal = [v % ROWS for v in mine]
    for r in range(ROWS):
        low, high = jnp.int32(0), jnp.int32(0)
        for t in range(TILES):
            high = jnp.where(goal[t] == r, t, high)
            low = jnp.where(goal[TILES - 1 - t] == r, TILES - 1 - t, low)
        order[2 * r] = low
        order[2 * r + 1] = high
    for p in range(2):
        where_p, held = jnp.int32(0), jnp.int32(0)
        for t in range(TILES):
            where_p = jnp.where(mine[t] == p, t, where_p)
            held = jnp.where(mine[t] == p, 1, held)
        order[TILES + 2 * p] = where_p
        order[TILES + 2 * p + 1] = held

    pl.semaphore_wait(barrier, ROWS - 1 + 2 * (Q - 1))

    def head(c2):
        return panels.at[0, :, pl.ds(pl.multiple_of(c2 * W, W), W)]

    @pl.when(row == 1)
    def _():
        for d in range(1, ROWS):
            r2 = (row + d) % ROWS
            c2 = r2 % 2
            g2 = x + c2 * (y - x)
            o2 = y + c2 * (x - y)
            send(head(c2), b1.at[o2, g2], b1z_s, b1z_r, (r2, col))
        own = pltpu.make_async_copy(head(core), b1.at[o, g], loc.at[4])
        own.start()
        own.wait()

    def scatter(h):
        for d in (2, 1, 3):
            send(eighth(h, (g + d) % Q), lg.at[h, :, o, g], lg_s, lg_r.at[h], at_g(d))

    scatter(0)

    rhs_in.wait()
    for p in range(2):
        mm[p] = rhs_v[order[TILES + 2 * p]] * order[TILES + 2 * p + 1].astype(F32)
    half = pl.ds(pl.multiple_of(core * W, W), W)
    other = pl.ds(pl.multiple_of((1 - core) * W, W), W)
    send(mm.at[:, other], xb, mx_s, mx_r, sibling)

    def reorder(t, carry):
        send_v[t] = rhs_v[order[t]]
        return carry

    lax.fori_loop(0, TILES, reorder, 0)

    @pl.when(row != 1)
    def _():
        landed(b1.at[o, g], b1z_s, b1z_r, (1, col))

    for d in range(1, Q):
        send(b1.at[o, g], b1.at[o, g], b1g_s, b1g_r, at_g(d))
    scatter(1)

    left_here(mm.at[:, other], mx_s)
    landed(xb, mx_s, mx_r, sibling)
    mm[:, half] = mm[:, half] + xb[...]

    def piece(zz):
        return pl.ds(pl.multiple_of(core * W + zz * (W // Q), W // Q), W // Q)

    for d in (2, 1, 3):
        send(mm.at[:, piece((z + d) % Q)], rs.at[d - 1], rs_s, rs_r, at_z(d))

    def gathered(h):
        own_l[h].wait()
        landed(lg.at[h, :, o, pl.ds(0, Q - 1)], lg_s, lg_r.at[h], at_g(1))

    def legs(p):
        return ((1, 0), (Q - 1, 2)) if p == 0 else ((Q - 1, 1), (1, 2))

    def first_leg(h):
        for p in range(2):
            for d, n in legs(p):
                send(lg.at[h, p, o], lg.at[h, p, o], lo_s, lo_r.at[h, n], at_o(d))

    def second_leg(h):
        for p in range(2):
            d = (1, Q - 1)[p]
            oo = (left_o, right_o)[p]
            landed(lg.at[h, p, oo], lo_s, lo_r.at[h, p], at_o(d))
            for gg in range(Q):
                part = lg.at[h, p, oo, gg]
                send(part, part, lo_s, lo_r.at[h, 2], at_o(d))

    def all_legs(h):
        landed(lg.at[h, 0], lo_s, lo_r.at[h, 2], at_o(1))

    landed(b1.at[o, pl.ds(0, Q - 1)], b1g_s, b1g_r, at_g(1))
    for d in (2, 1, 3):
        send(b1.at[o], b1.at[o], b1o_s, b1o_r, at_o(d))
    gathered(0)
    first_leg(0)

    landed(rs, rs_s, rs_r, at_z(1))
    rr[:, piece(z)] = mm[:, piece(z)] + (rs[0] + rs[1] + rs[2])
    for d in (2, 1, 3):
        send(rr.at[:, piece(z)], rr.at[:, piece(z)], ag_s, ag_r, at_z(d))

    gathered(1)

    landed(rs, ag_s, ag_r, at_z(1))
    send(rr.at[:, half], rr.at[:, half], rx_s, rx_r, sibling)

    for d in (4, 2, 6, 3, 5, 1, 7):
        send(send_v.at[pl.ds(2 * ((row + d) % ROWS), 2)], recv.at[pl.ds(2 * row, 2)], az_s, az_r, at_row(d))
    own_t = pltpu.make_async_copy(send_v.at[pl.ds(2 * row, 2)], recv.at[pl.ds(2 * row, 2)], loc.at[4])
    own_t.start()
    dinv_in.wait()
    landed(rr.at[:, other], rx_s, rx_r, sibling)

    def arrange(which, value):
        first_n[...] = value
        solved[which] = value

        def put(n, carry):
            oo, gg = n // Q, n % Q
            sg[g, which, pl.ds(pl.multiple_of(n * 32, 32), 32)] = first_n[
                pl.ds(pl.multiple_of(col_of(gg, oo) * 32, 32), 32)
            ]
            return carry

        lax.fori_loop(0, TILES, put, 0)

    def spread(p):
        for d, n in legs(p):
            send(sg.at[g, p], sg.at[g, p], sg_s, sg_r.at[n], at_g(d))

    def solve(which, block):
        return jnp.dot(dv[which], block, precision=lax.Precision.HIGHEST, preferred_element_type=F32)

    arrange(0, solve(0, rr[0]))
    spread(0)
    landed(b1.at[pl.ds(0, Q - 1)], b1o_s, b1o_r, at_o(1))
    left_here(rs, rs_s)
    mm[0, half] = rr[1, half] - dot_t(b1[...].reshape(NB, W), sg[g, 0])
    send(mm.at[0, half], mm.at[0, half], hx_s, hx_r, sibling)
    landed(mm.at[0, other], hx_s, hx_r, sibling)
    arrange(1, solve(1, mm[0]))
    spread(1)

    def split_solved(gg, p):
        hi, lo = split(sg[gg, p])
        sh[gg, pl.ds(p * NB, NB)] = hi
        sl[gg, pl.ds(p * NB, NB)] = lo

    def spread_on(p):
        d = (1, Q - 1)[p]
        gg = (left_g, right_g)[p]
        landed(sg.at[gg, p], sg_s, sg_r.at[p], at_g(d))
        send(sg.at[gg, p], sg.at[gg, p], sg_s, sg_r.at[2], at_g(d))

    spread_on(0)
    second_leg(0)
    first_leg(1)
    spread_on(1)
    for p in range(2):
        split_solved(g, p)
        split_solved((left_g, right_g)[p], p)
    landed(sg.at[pl.ds(0, 2)], sg_s, sg_r.at[2], at_g(1))
    for p in range(2):
        split_solved((right_g, left_g)[p], p)
        split_solved(far_g, p)

    def tile_step(i, carry):
        def turn(n, inner):
            p = n // Q
            keep = jnp.where((i == 0) & (g == 0) & (row <= p), 0.0, 1.0).astype(F32)
            part = lg[i // 2, p, n % Q, :, :, pl.ds(pl.multiple_of((i % 2) * NB, NB), NB)].reshape(4 * 32, NB)
            hi, lo = split(part.T * keep)
            at = pl.ds(pl.multiple_of(n * 128, 128), 128)
            lh[:, at] = hi
            ll[:, at] = lo
            return inner

        lax.fori_loop(0, 2 * Q, turn, 0)

        def dest_step(m, inner):
            d = (m + 2) % Q
            gg = (g + d) % Q
            a, b = lh[...], sh[gg]
            acc = jnp.dot(a, b, preferred_element_type=F32)
            acc += jnp.dot(a, sl[gg], preferred_element_type=F32)
            acc += jnp.dot(ll[...], b, preferred_element_type=F32)

            @pl.when(d != 0)
            def _():
                n = Q * d - Q + i
                rhs_v[n] = acc
                send(rhs_v.at[n], upd.at[Q * g + i], u_s, u_r, (row, col_of(gg, o)))

            @pl.when(d == 0)
            def _():
                upd[Q * g + i] = acc

            return inner

        lax.fori_loop(0, Q, dest_step, 0)
        return carry

    tbv_in = pltpu.make_async_copy(tbv_hbm, tbv, loc.at[0])
    tbv_in.start()
    all_legs(0)
    lax.fori_loop(0, 1, tile_step, 0)
    second_leg(1)
    lax.fori_loop(1, 2, tile_step, 0)
    all_legs(1)
    lax.fori_loop(2, Q, tile_step, 0)

    tbv_in.wait()
    ids = tbv[...]
    every = lax.broadcasted_iota(jnp.int32, (TILES, ROWS * TILES), 1)
    want = lax.broadcasted_iota(jnp.int32, (TILES, ROWS * TILES), 0) * ROWS + row
    where_is = jnp.sum(jnp.where(ids == want, every, 0), axis=1, keepdims=True)
    before = (every < where_is) & (ids % ROWS == row)
    count = jnp.sum(before.astype(jnp.int32), axis=1, keepdims=True)
    count = jnp.broadcast_to(count, (TILES, ROWS * TILES))
    placing[...] = count

    own_t.wait()
    landed(send_v.at[pl.ds(0, TILES - 2)], az_s, az_r, sibling)
    left_here(send_v.at[pl.ds(0, TILES - 2)], az_s)
    left_here(lg.at[0, 0, pl.ds(0, Q - 1)], lg_s)
    left_here(rhs_v.at[pl.ds(0, 3 * Q)], lo_s)
    left_here(b1.at[0, pl.ds(0, Q - 1)], b1g_s)
    left_here(b1.at[pl.ds(0, Q - 1)], b1o_s)
    left_here(rs, ag_s)
    left_here(rr.at[:, half], rx_s)
    left_here(mm.at[0, half], hx_s)
    left_here(rhs_v.at[pl.ds(0, 6)], sg_s)

    @pl.when(row == 1)
    def _():
        left_here(send_v.at[0, pl.ds(0, 32 * (ROWS - 1))], b1z_s)

    left_here(rhs_v.at[pl.ds(0, 3 * Q)], u_s)
    landed(rhs_v.at[pl.ds(0, 3 * Q)], u_s, u_r, at_g(1))


def finish_body(placing, recv, upd, solved, out, solved_out, stage, sems, sol_sem):
    sol = pltpu.make_async_copy(solved, solved_out, sol_sem)
    sol.start()
    depth = stage.shape[0]

    def put(b):
        return pltpu.make_async_copy(stage.at[b % depth], out.at[b], sems.at[b % depth])

    for b in range(TILES):
        if b >= depth:
            put(b - depth).wait()
        stage[b % depth] = recv[placing[b, 0]] - upd[b]
        put(b).start()
    for b in range(TILES - depth, TILES):
        put(b).wait()
    sol.wait()


def shards(rhs_atlas, tile_block, panels, diag_inverse):
    dma = pltpu.SemaphoreType.DMA
    hbm = pl.BlockSpec(memory_space=pltpu.HBM)
    vmem = pl.BlockSpec(memory_space=pltpu.VMEM)
    tiles = (TILES, NB, W)
    recv, upd, solved, placing = pl.pallas_call(
        exchange,
        out_shape=(
            pltpu.VMEM(tiles, F32),
            pltpu.VMEM(tiles, F32),
            pltpu.VMEM((2, NB, W), F32),
            pltpu.VMEM((TILES, ROWS * TILES), jnp.int32),
        ),
        in_specs=[hbm] * 5,
        out_specs=(vmem, vmem, vmem, vmem),
        scratch_shapes=[
            pltpu.VMEM(tiles, F32),
            pltpu.VMEM(tiles, F32),
            pltpu.VMEM((2, 2, Q, Q, 32, HB), F32),
            pltpu.VMEM((Q, 2, NB, W), F32),
            pltpu.VMEM((Q, 2 * NB, W), BF16),
            pltpu.VMEM((Q, 2 * NB, W), BF16),
            pltpu.VMEM((NB, 2 * NB), BF16),
            pltpu.VMEM((NB, 2 * NB), BF16),
            pltpu.VMEM((2, NB, W), F32),
            pltpu.VMEM((2, W, W), F32),
            pltpu.VMEM((Q - 1, 2, W // Q, W), F32),
            pltpu.VMEM((2, NB, W), F32),
            pltpu.VMEM((Q, Q, 32, W), F32),
            pltpu.VMEM((2, NB, NB), F32),
            pltpu.VMEM((NB, W), F32),
            pltpu.SMEM((ROWS * TILES,), jnp.int32),
            pltpu.VMEM((1, ROWS * TILES), jnp.int32),
            pltpu.SMEM((TILES + 4,), jnp.int32),
            dma((5,)), dma(()), dma(()), dma(()), dma(()), dma(()), dma(()), dma(()), dma((2,)), dma(()), dma((2, 3)),
            dma(()), dma(()), dma(()), dma(()), dma(()), dma(()), dma(()), dma(()), dma(()), dma(()), dma(()), dma(()),
            dma(()), dma((3,)), dma(()), dma(()),
        ],
        compiler_params=pltpu.CompilerParams(
            collective_id=0, has_side_effects=True, vmem_limit_bytes=44 * 1024 * 1024
        ),
        name="exchange",
    )(tile_block, tile_block.reshape(1, -1), rhs_atlas.reshape(tiles), panels, diag_inverse)

    trailing, solved = pl.pallas_call(
        finish_body,
        out_shape=(jax.ShapeDtypeStruct(tiles, F32), jax.ShapeDtypeStruct((2, NB, W), F32)),
        in_specs=[vmem, vmem, vmem, vmem],
        out_specs=(hbm, hbm),
        scratch_shapes=[pltpu.VMEM((8, NB, W), F32), dma((8,)), dma(())],
        compiler_params=pltpu.CompilerParams(vmem_limit_bytes=6 * 1024 * 1024),
        name="finish",
    )(placing, recv, upd, solved)
    return solved, trailing.reshape(TILES * NB, W)


def solution(mesh):
    placed = (P("row", "col"), P(), P(None, "col", "row"), P())
    return jax.shard_map(
        shards,
        mesh=mesh,
        in_specs=placed,
        out_specs=(P(None, None, "col"), P("row", "col")),
        check_vma=False,
    )
```

```python
import jax
import jax.numpy as jnp
from jax import lax
from jax.experimental import pallas as pl
from jax.experimental.pallas import tpu as pltpu
from jax.sharding import PartitionSpec as P

MESH = pl.DeviceIdType.MESH
F32 = jnp.float32
BF16 = jnp.bfloat16
NB = 512
W = 256
ROWS = 8
TILES = 16
Q = 4
HB = 2 * NB


def split(v):
    hi = v.astype(BF16)
    return hi, (v - hi.astype(F32)).astype(BF16)


def dot_t(a, b):
    return lax.dot_general(
        a, b, (((0,), (0,)), ((), ())), precision=lax.Precision.HIGHEST, preferred_element_type=F32
    )


def exchange(
    tb_hbm, tbv_hbm, rhs, panels, dinv,
    recv, upd, solved, placing,
    rhs_v, send_v, lg, sg, sh, sl, lh, ll, mm, xb, rs, rr, b1, dv, first_n, tb, tbv, order,
    loc, b1z_s, b1z_r, b1g_s, b1g_r, b1o_r, lg_r, lo_s, lo_r,
    mx_s, mx_r, rs_s, rs_r, ag_r, rx_r, hx_r, az_s, az_r,
    sg_s, sg_r, u_s, u_r,
):
    row = lax.axis_index("row")
    col = lax.axis_index("col")
    z, core = row // 2, row % 2
    x, y = col // Q, col % Q
    g = x + core * (y - x)
    o = y + core * (x - y)
    left_g, right_g, far_g = (g + 3) % Q, (g + 1) % Q, (g + 2) % Q
    left_o, right_o, far_o = (o + 3) % Q, (o + 1) % Q, (o + 2) % Q

    def col_of(gg, oo):
        return gg * Q + oo + core * ((oo * Q + gg) - (gg * Q + oo))

    def at_g(d):
        return (row, col_of((g + d) % Q, o))

    def at_o(d):
        return (row, col_of(g, (o + d) % Q))

    def at_z(d):
        return (((z + d) % Q) * 2 + core, col)

    def at_row(d):
        return ((row + d) % ROWS, col)

    sibling = (z * 2 + 1 - core, col)

    def remote(src, dst, ss, rsem, dev):
        return pltpu.make_async_remote_copy(
            src_ref=src, dst_ref=dst, send_sem=ss, recv_sem=rsem, device_id=dev, device_id_type=MESH
        )

    def landed(ref, ss, rsem, dev):
        remote(ref, ref, ss, rsem, dev).wait_recv()

    def send(src, dst, ss, rsem, dev):
        remote(src, dst, ss, rsem, dev).start()

    def left_here(ref, ss):
        remote(ref, ref, ss, ss, sibling).wait_send()

    def eighth(h, gg):
        return panels.at[:, :, pl.ds(pl.multiple_of(gg * (Q * NB) + h * HB, HB), HB)]

    barrier = pltpu.get_barrier_semaphore()
    for d in range(1, ROWS):
        pl.semaphore_signal(barrier, inc=1, device_id=at_row(d), device_id_type=MESH)
    for d in range(1, Q):
        pl.semaphore_signal(barrier, inc=1, device_id=at_g(d), device_id_type=MESH)
        pl.semaphore_signal(barrier, inc=1, device_id=at_o(d), device_id_type=MESH)

    tb_in = pltpu.make_async_copy(tb_hbm, tb, loc.at[4])
    tb_in.start()
    rhs_in = pltpu.make_async_copy(rhs, rhs_v, loc.at[0])
    rhs_in.start()
    own_l = [pltpu.make_async_copy(eighth(h, g), lg.at[h, :, o, g], loc.at[1 + h]) for h in range(2)]
    for c in own_l:
        c.start()
    dinv_in = pltpu.make_async_copy(dinv, dv, loc.at[3])
    dinv_in.start()
    tb_in.wait()

    mine = [tb[row * TILES + t] for t in range(TILES)]
    goal = [v % ROWS for v in mine]
    for r in range(ROWS):
        low, high = jnp.int32(0), jnp.int32(0)
        for t in range(TILES):
            high = jnp.where(goal[t] == r, t, high)
            low = jnp.where(goal[TILES - 1 - t] == r, TILES - 1 - t, low)
        order[2 * r] = low
        order[2 * r + 1] = high
    for p in range(2):
        where_p, held = jnp.int32(0), jnp.int32(0)
        for t in range(TILES):
            where_p = jnp.where(mine[t] == p, t, where_p)
            held = jnp.where(mine[t] == p, 1, held)
        order[TILES + 2 * p] = where_p
        order[TILES + 2 * p + 1] = held

    pl.semaphore_wait(barrier, ROWS - 1 + 2 * (Q - 1))

    def head(c2):
        return panels.at[0, :, pl.ds(pl.multiple_of(c2 * W, W), W)]

    @pl.when(row == 1)
    def _():
        for d in range(1, ROWS):
            r2 = (row + d) % ROWS
            c2 = r2 % 2
            g2 = x + c2 * (y - x)
            o2 = y + c2 * (x - y)
            send(head(c2), b1.at[o2, g2], b1z_s, b1z_r, (r2, col))
        own = pltpu.make_async_copy(head(core), b1.at[o, g], loc.at[4])
        own.start()
        own.wait()

    def scatter(h):
        for d in (2, 1, 3):
            send(eighth(h, (g + d) % Q), lg.at[h, :, o, g], lo_s, lg_r.at[h], at_g(d))

    scatter(0)

    rhs_in.wait()
    for p in range(2):
        mm[p] = rhs_v[order[TILES + 2 * p]] * order[TILES + 2 * p + 1].astype(F32)
    half = pl.ds(pl.multiple_of(core * W, W), W)
    other = pl.ds(pl.multiple_of((1 - core) * W, W), W)
    send(mm.at[:, other], xb, mx_s, mx_r, sibling)

    def reorder(t, carry):
        send_v[t] = rhs_v[order[t]]
        return carry

    lax.fori_loop(0, TILES, reorder, 0)

    @pl.when(row != 1)
    def _():
        landed(b1.at[o, g], b1z_s, b1z_r, (1, col))

    for d in range(1, Q):
        send(b1.at[o, g], b1.at[o, g], b1g_s, b1g_r, at_g(d))
    scatter(1)

    left_here(mm.at[:, other], mx_s)
    landed(xb, mx_s, mx_r, sibling)
    mm[:, half] = mm[:, half] + xb[...]

    def piece(zz):
        return pl.ds(pl.multiple_of(core * W + zz * (W // Q), W // Q), W // Q)

    for d in (2, 1, 3):
        send(mm.at[:, piece((z + d) % Q)], rs.at[d - 1], rs_s, rs_r, at_z(d))

    def gathered(h):
        own_l[h].wait()
        landed(lg.at[h, :, o, pl.ds(0, Q - 1)], lo_s, lg_r.at[h], at_g(1))

    def legs(p):
        return ((1, 0), (Q - 1, 2)) if p == 0 else ((Q - 1, 1), (1, 2))

    def first_leg(h):
        for p in range(2):
            for d, n in legs(p):
                send(lg.at[h, p, o], lg.at[h, p, o], lo_s, lo_r.at[h, n], at_o(d))

    def second_leg(h):
        for p in range(2):
            d = (1, Q - 1)[p]
            oo = (left_o, right_o)[p]
            landed(lg.at[h, p, oo], lo_s, lo_r.at[h, p], at_o(d))
            for gg in range(Q):
                part = lg.at[h, p, oo, gg]
                send(part, part, lo_s, lo_r.at[h, 2], at_o(d))

    def all_legs(h):
        landed(lg.at[h, 0], lo_s, lo_r.at[h, 2], at_o(1))

    landed(b1.at[o, pl.ds(0, Q - 1)], b1g_s, b1g_r, at_g(1))
    for d in (2, 1, 3):
        send(b1.at[o], b1.at[o], sg_s, b1o_r, at_o(d))
    gathered(0)
    first_leg(0)

    landed(rs, rs_s, rs_r, at_z(1))
    rr[:, piece(z)] = mm[:, piece(z)] + (rs[0] + rs[1] + rs[2])
    for d in (2, 1, 3):
        send(rr.at[:, piece(z)], rr.at[:, piece(z)], sg_s, ag_r, at_z(d))

    gathered(1)

    landed(rs, sg_s, ag_r, at_z(1))
    send(rr.at[:, half], rr.at[:, half], sg_s, rx_r, sibling)

    for d in (4, 2, 6, 3, 5, 1, 7):
        send(send_v.at[pl.ds(2 * ((row + d) % ROWS), 2)], recv.at[pl.ds(2 * row, 2)], az_s, az_r, at_row(d))
    own_t = pltpu.make_async_copy(send_v.at[pl.ds(2 * row, 2)], recv.at[pl.ds(2 * row, 2)], loc.at[4])
    own_t.start()
    dinv_in.wait()
    landed(rr.at[:, other], sg_s, rx_r, sibling)

    def arrange(which, value):
        first_n[...] = value
        solved[which] = value

        def put(n, carry):
            oo, gg = n // Q, n % Q
            sg[g, which, pl.ds(pl.multiple_of(n * 32, 32), 32)] = first_n[
                pl.ds(pl.multiple_of(col_of(gg, oo) * 32, 32), 32)
            ]
            return carry

        lax.fori_loop(0, TILES, put, 0)

    def spread(p):
        for d, n in legs(p):
            send(sg.at[g, p], sg.at[g, p], sg_s, sg_r.at[n], at_g(d))

    def solve(which, block):
        return jnp.dot(dv[which], block, precision=lax.Precision.HIGHEST, preferred_element_type=F32)

    arrange(0, solve(0, rr[0]))
    spread(0)
    landed(b1.at[pl.ds(0, Q - 1)], sg_s, b1o_r, at_o(1))
    left_here(rs, rs_s)
    mm[0, half] = rr[1, half] - dot_t(b1[...].reshape(NB, W), sg[g, 0])
    send(mm.at[0, half], mm.at[0, half], sg_s, hx_r, sibling)
    landed(mm.at[0, other], sg_s, hx_r, sibling)
    arrange(1, solve(1, mm[0]))
    spread(1)

    def split_solved(gg, p):
        hi, lo = split(sg[gg, p])
        sh[gg, pl.ds(p * NB, NB)] = hi
        sl[gg, pl.ds(p * NB, NB)] = lo

    def spread_on(p):
        d = (1, Q - 1)[p]
        gg = (left_g, right_g)[p]
        landed(sg.at[gg, p], sg_s, sg_r.at[p], at_g(d))
        send(sg.at[gg, p], sg.at[gg, p], sg_s, sg_r.at[2], at_g(d))

    spread_on(0)
    second_leg(0)
    first_leg(1)
    spread_on(1)
    for p in range(2):
        split_solved(g, p)
        split_solved((left_g, right_g)[p], p)
    landed(sg.at[pl.ds(0, 2)], sg_s, sg_r.at[2], at_g(1))
    for p in range(2):
        split_solved((right_g, left_g)[p], p)
        split_solved(far_g, p)

    def tile_step(i, carry):
        def turn(n, inner):
            p = n // Q
            keep = jnp.where((i == 0) & (g == 0) & (row <= p), 0.0, 1.0).astype(F32)
            part = lg[i // 2, p, n % Q, :, :, pl.ds(pl.multiple_of((i % 2) * NB, NB), NB)].reshape(4 * 32, NB)
            hi, lo = split(part.T * keep)
            at = pl.ds(pl.multiple_of(n * 128, 128), 128)
            lh[:, at] = hi
            ll[:, at] = lo
            return inner

        lax.fori_loop(0, 2 * Q, turn, 0)

        def dest_step(m, inner):
            d = (m + 2) % Q
            gg = (g + d) % Q
            a, b = lh[...], sh[gg]
            acc = jnp.dot(a, b, preferred_element_type=F32)
            acc += jnp.dot(a, sl[gg], preferred_element_type=F32)
            acc += jnp.dot(ll[...], b, preferred_element_type=F32)

            @pl.when(d != 0)
            def _():
                n = Q * d - Q + i
                rhs_v[n] = acc
                send(rhs_v.at[n], upd.at[Q * g + i], u_s, u_r, (row, col_of(gg, o)))

            @pl.when(d == 0)
            def _():
                upd[Q * g + i] = acc

            return inner

        lax.fori_loop(0, Q, dest_step, 0)
        return carry

    tbv_in = pltpu.make_async_copy(tbv_hbm, tbv, loc.at[0])
    tbv_in.start()
    all_legs(0)
    lax.fori_loop(0, 1, tile_step, 0)
    second_leg(1)
    lax.fori_loop(1, 2, tile_step, 0)
    all_legs(1)
    lax.fori_loop(2, Q, tile_step, 0)

    tbv_in.wait()
    ids = tbv[...]
    every = lax.broadcasted_iota(jnp.int32, (TILES, ROWS * TILES), 1)
    want = lax.broadcasted_iota(jnp.int32, (TILES, ROWS * TILES), 0) * ROWS + row
    where_is = jnp.sum(jnp.where(ids == want, every, 0), axis=1, keepdims=True)
    before = (every < where_is) & (ids % ROWS == row)
    count = jnp.sum(before.astype(jnp.int32), axis=1, keepdims=True)
    count = jnp.broadcast_to(count, (TILES, ROWS * TILES))
    placing[...] = count

    own_t.wait()
    landed(send_v.at[pl.ds(0, TILES - 2)], az_s, az_r, sibling)
    left_here(send_v.at[pl.ds(0, TILES - 2)], az_s)
    left_here(send_v.at[pl.ds(0, 15)], lo_s)
    left_here(b1.at[0, pl.ds(0, Q - 1)], b1g_s)
    left_here(send_v.at[pl.ds(0, 9)], sg_s)

    @pl.when(row == 1)
    def _():
        left_here(send_v.at[0, pl.ds(0, 32 * (ROWS - 1))], b1z_s)

    left_here(rhs_v.at[pl.ds(0, 3 * Q)], u_s)
    landed(rhs_v.at[pl.ds(0, 3 * Q)], u_s, u_r, at_g(1))


def finish_body(placing, recv, upd, solved, out, solved_out, stage, sems, sol_sem):
    sol = pltpu.make_async_copy(solved, solved_out, sol_sem)
    sol.start()
    depth = stage.shape[0]
    places = [placing[b, 0] for b in range(TILES)]

    def put(b):
        return pltpu.make_async_copy(stage.at[b % depth], out.at[b], sems.at[b % depth])

    for b in range(TILES):
        if b >= depth:
            put(b - depth).wait()
        stage[b % depth] = recv[places[b]] - upd[b]
        put(b).start()
    for b in range(TILES - depth, TILES):
        put(b).wait()
    sol.wait()


def shards(rhs_atlas, tile_block, panels, diag_inverse):
    dma = pltpu.SemaphoreType.DMA
    hbm = pl.BlockSpec(memory_space=pltpu.HBM)
    vmem = pl.BlockSpec(memory_space=pltpu.VMEM)
    tiles = (TILES, NB, W)
    recv, upd, solved, placing = pl.pallas_call(
        exchange,
        out_shape=(
            pltpu.VMEM(tiles, F32),
            pltpu.VMEM(tiles, F32),
            pltpu.VMEM((2, NB, W), F32),
            pltpu.VMEM((TILES, ROWS * TILES), jnp.int32),
        ),
        in_specs=[hbm] * 5,
        out_specs=(vmem, vmem, vmem, vmem),
        scratch_shapes=[
            pltpu.VMEM(tiles, F32),
            pltpu.VMEM(tiles, F32),
            pltpu.VMEM((2, 2, Q, Q, 32, HB), F32),
            pltpu.VMEM((Q, 2, NB, W), F32),
            pltpu.VMEM((Q, 2 * NB, W), BF16),
            pltpu.VMEM((Q, 2 * NB, W), BF16),
            pltpu.VMEM((NB, 2 * NB), BF16),
            pltpu.VMEM((NB, 2 * NB), BF16),
            pltpu.VMEM((2, NB, W), F32),
            pltpu.VMEM((2, W, W), F32),
            pltpu.VMEM((Q - 1, 2, W // Q, W), F32),
            pltpu.VMEM((2, NB, W), F32),
            pltpu.VMEM((Q, Q, 32, W), F32),
            pltpu.VMEM((2, NB, NB), F32),
            pltpu.VMEM((NB, W), F32),
            pltpu.SMEM((ROWS * TILES,), jnp.int32),
            pltpu.VMEM((1, ROWS * TILES), jnp.int32),
            pltpu.SMEM((TILES + 4,), jnp.int32),
            dma((5,)), dma(()), dma(()), dma(()), dma(()), dma(()), dma((2,)), dma(()), dma((2, 3)),
            dma(()), dma(()), dma(()), dma(()), dma(()), dma(()), dma(()), dma(()), dma(()),
            dma(()), dma((3,)), dma(()), dma(()),
        ],
        compiler_params=pltpu.CompilerParams(
            collective_id=0, has_side_effects=True, vmem_limit_bytes=44 * 1024 * 1024
        ),
        name="exchange",
    )(tile_block, tile_block.reshape(1, -1), rhs_atlas.reshape(tiles), panels, diag_inverse)

    trailing, solved = pl.pallas_call(
        finish_body,
        out_shape=(jax.ShapeDtypeStruct(tiles, F32), jax.ShapeDtypeStruct((2, NB, W), F32)),
        in_specs=[vmem, vmem, vmem, vmem],
        out_specs=(hbm, hbm),
        scratch_shapes=[pltpu.VMEM((8, NB, W), F32), dma((8,)), dma(())],
        compiler_params=pltpu.CompilerParams(vmem_limit_bytes=6 * 1024 * 1024),
        name="finish",
    )(placing, recv, upd, solved)
    return solved, trailing.reshape(TILES * NB, W)


def solution(mesh):
    placed = (P("row", "col"), P(), P(None, "col", "row"), P())
    return jax.shard_map(
        shards,
        mesh=mesh,
        in_specs=placed,
        out_specs=(P(None, None, "col"), P("row", "col")),
        check_vma=False,
    )
```

```python
import jax
import jax.numpy as jnp
from jax import lax
from jax.experimental import pallas as pl
from jax.experimental.pallas import tpu as pltpu
from jax.sharding import PartitionSpec as P

MESH = pl.DeviceIdType.MESH
F32 = jnp.float32
BF16 = jnp.bfloat16
NB = 512
W = 256
ROWS = 8
TILES = 16
Q = 4
HB = 2 * NB


def split(v):
    hi = v.astype(BF16)
    return hi, (v - hi.astype(F32)).astype(BF16)


def dot_t(a, b):
    return lax.dot_general(
        a, b, (((0,), (0,)), ((), ())), precision=lax.Precision.HIGHEST, preferred_element_type=F32
    )


def exchange(
    tb_hbm, tbv_hbm, rhs, panels, dinv,
    recv, upd, solved, placing,
    rhs_v, send_v, lg, sg, sh, sl, lh, ll, mm, xb, rs, rr, b1, dv, first_n, tb, tbv, order,
    loc, b1z_s, b1z_r, b1g_s, b1g_r, b1o_r, lg_r, lo_s, lo_r,
    mx_s, mx_r, rs_s, rs_r, ag_r, rx_r, hx_r, az_s, az_r,
    sg_s, sg_r, u_s, u_r,
):
    row = lax.axis_index("row")
    col = lax.axis_index("col")
    z, core = row // 2, row % 2
    x, y = col // Q, col % Q
    g = x + core * (y - x)
    o = y + core * (x - y)
    left_g, right_g, far_g = (g + 3) % Q, (g + 1) % Q, (g + 2) % Q
    left_o, right_o, far_o = (o + 3) % Q, (o + 1) % Q, (o + 2) % Q

    def col_of(gg, oo):
        return gg * Q + oo + core * ((oo * Q + gg) - (gg * Q + oo))

    def at_g(d):
        return (row, col_of((g + d) % Q, o))

    def at_o(d):
        return (row, col_of(g, (o + d) % Q))

    def at_z(d):
        return (((z + d) % Q) * 2 + core, col)

    def at_row(d):
        return ((row + d) % ROWS, col)

    sibling = (z * 2 + 1 - core, col)

    def remote(src, dst, ss, rsem, dev):
        return pltpu.make_async_remote_copy(
            src_ref=src, dst_ref=dst, send_sem=ss, recv_sem=rsem, device_id=dev, device_id_type=MESH
        )

    def landed(ref, ss, rsem, dev):
        remote(ref, ref, ss, rsem, dev).wait_recv()

    def send(src, dst, ss, rsem, dev):
        remote(src, dst, ss, rsem, dev).start()

    def left_here(ref, ss):
        remote(ref, ref, ss, ss, sibling).wait_send()

    def eighth(h, gg):
        return panels.at[:, :, pl.ds(pl.multiple_of(gg * (Q * NB) + h * HB, HB), HB)]

    barrier = pltpu.get_barrier_semaphore()
    for d in range(1, ROWS):
        pl.semaphore_signal(barrier, inc=1, device_id=at_row(d), device_id_type=MESH)
    for d in range(1, Q):
        pl.semaphore_signal(barrier, inc=1, device_id=at_g(d), device_id_type=MESH)
        pl.semaphore_signal(barrier, inc=1, device_id=at_o(d), device_id_type=MESH)

    tb_in = pltpu.make_async_copy(tb_hbm, tb, loc.at[4])
    tb_in.start()
    rhs_in = pltpu.make_async_copy(rhs, rhs_v, loc.at[0])
    rhs_in.start()
    own_l = [pltpu.make_async_copy(eighth(h, g), lg.at[h, :, o, g], loc.at[1 + h]) for h in range(2)]
    for c in own_l:
        c.start()
    dinv_in = pltpu.make_async_copy(dinv, dv, loc.at[3])
    dinv_in.start()
    tb_in.wait()

    mine = [tb[row * TILES + t] for t in range(TILES)]
    goal = [v % ROWS for v in mine]
    for r in range(ROWS):
        low, high = jnp.int32(0), jnp.int32(0)
        for t in range(TILES):
            high = jnp.where(goal[t] == r, t, high)
            low = jnp.where(goal[TILES - 1 - t] == r, TILES - 1 - t, low)
        order[2 * r] = low
        order[2 * r + 1] = high
    for p in range(2):
        where_p, held = jnp.int32(0), jnp.int32(0)
        for t in range(TILES):
            where_p = jnp.where(mine[t] == p, t, where_p)
            held = jnp.where(mine[t] == p, 1, held)
        order[TILES + 2 * p] = where_p
        order[TILES + 2 * p + 1] = held

    pl.semaphore_wait(barrier, ROWS - 1 + 2 * (Q - 1))

    def head(c2):
        return panels.at[0, :, pl.ds(pl.multiple_of(c2 * W, W), W)]

    @pl.when(row == 1)
    def _():
        for d in range(1, ROWS):
            r2 = (row + d) % ROWS
            c2 = r2 % 2
            g2 = x + c2 * (y - x)
            o2 = y + c2 * (x - y)
            send(head(c2), b1.at[o2, g2], b1z_s, b1z_r, (r2, col))
        own = pltpu.make_async_copy(head(core), b1.at[o, g], loc.at[4])
        own.start()
        own.wait()

    def scatter(h):
        for d in (2, 1, 3):
            send(eighth(h, (g + d) % Q), lg.at[h, :, o, g], lo_s, lg_r.at[h], at_g(d))

    scatter(0)

    rhs_in.wait()
    for p in range(2):
        mm[p] = rhs_v[order[TILES + 2 * p]] * order[TILES + 2 * p + 1].astype(F32)
    half = pl.ds(pl.multiple_of(core * W, W), W)
    other = pl.ds(pl.multiple_of((1 - core) * W, W), W)
    send(mm.at[:, other], xb, mx_s, mx_r, sibling)

    def reorder(t, carry):
        send_v[t] = rhs_v[order[t]]
        return carry


    @pl.when(row != 1)
    def _():
        landed(b1.at[o, g], b1z_s, b1z_r, (1, col))

    for d in range(1, Q):
        send(b1.at[o, g], b1.at[o, g], b1g_s, b1g_r, at_g(d))
    scatter(1)

    left_here(mm.at[:, other], mx_s)
    landed(xb, mx_s, mx_r, sibling)
    mm[:, half] = mm[:, half] + xb[...]

    def piece(zz):
        return pl.ds(pl.multiple_of(core * W + zz * (W // Q), W // Q), W // Q)

    for d in (2, 1, 3):
        send(mm.at[:, piece((z + d) % Q)], rs.at[d - 1], rs_s, rs_r, at_z(d))

    lax.fori_loop(0, TILES, reorder, 0)

    def gathered(h):
        own_l[h].wait()
        landed(lg.at[h, :, o, pl.ds(0, Q - 1)], lo_s, lg_r.at[h], at_g(1))

    def legs(p):
        return ((1, 0), (Q - 1, 2)) if p == 0 else ((Q - 1, 1), (1, 2))

    def first_leg(h):
        for p in range(2):
            for d, n in legs(p):
                send(lg.at[h, p, o], lg.at[h, p, o], lo_s, lo_r.at[h, n], at_o(d))

    def second_leg(h):
        for p in range(2):
            d = (1, Q - 1)[p]
            oo = (left_o, right_o)[p]
            landed(lg.at[h, p, oo], lo_s, lo_r.at[h, p], at_o(d))
            for gg in range(Q):
                part = lg.at[h, p, oo, gg]
                send(part, part, lo_s, lo_r.at[h, 2], at_o(d))

    def all_legs(h):
        landed(lg.at[h, 0], lo_s, lo_r.at[h, 2], at_o(1))

    landed(b1.at[o, pl.ds(0, Q - 1)], b1g_s, b1g_r, at_g(1))
    for d in (2, 1, 3):
        send(b1.at[o], b1.at[o], sg_s, b1o_r, at_o(d))
    gathered(0)
    first_leg(0)

    landed(rs, rs_s, rs_r, at_z(1))
    rr[:, piece(z)] = mm[:, piece(z)] + (rs[0] + rs[1] + rs[2])
    for d in (2, 1, 3):
        send(rr.at[:, piece(z)], rr.at[:, piece(z)], sg_s, ag_r, at_z(d))

    gathered(1)

    landed(rs, sg_s, ag_r, at_z(1))
    send(rr.at[:, half], rr.at[:, half], sg_s, rx_r, sibling)

    for d in (4, 2, 6, 3, 5, 1, 7):
        send(send_v.at[pl.ds(2 * ((row + d) % ROWS), 2)], recv.at[pl.ds(2 * row, 2)], az_s, az_r, at_row(d))
    own_t = pltpu.make_async_copy(send_v.at[pl.ds(2 * row, 2)], recv.at[pl.ds(2 * row, 2)], loc.at[4])
    own_t.start()
    dinv_in.wait()
    landed(rr.at[:, other], sg_s, rx_r, sibling)

    def arrange(which, value):
        first_n[...] = value
        solved[which] = value

        def put(n, carry):
            oo, gg = n // Q, n % Q
            sg[g, which, pl.ds(pl.multiple_of(n * 32, 32), 32)] = first_n[
                pl.ds(pl.multiple_of(col_of(gg, oo) * 32, 32), 32)
            ]
            return carry

        lax.fori_loop(0, TILES, put, 0)

    def spread(p):
        for d, n in legs(p):
            send(sg.at[g, p], sg.at[g, p], sg_s, sg_r.at[n], at_g(d))

    def solve(which, block):
        return jnp.dot(dv[which], block, precision=lax.Precision.HIGHEST, preferred_element_type=F32)

    arrange(0, solve(0, rr[0]))
    spread(0)
    landed(b1.at[pl.ds(0, Q - 1)], sg_s, b1o_r, at_o(1))
    left_here(rs, rs_s)
    mm[0, half] = rr[1, half] - dot_t(b1[...].reshape(NB, W), sg[g, 0])
    send(mm.at[0, half], mm.at[0, half], sg_s, hx_r, sibling)
    landed(mm.at[0, other], sg_s, hx_r, sibling)
    arrange(1, solve(1, mm[0]))
    spread(1)

    def split_solved(gg, p):
        hi, lo = split(sg[gg, p])
        sh[gg, pl.ds(p * NB, NB)] = hi
        sl[gg, pl.ds(p * NB, NB)] = lo

    def spread_on(p):
        d = (1, Q - 1)[p]
        gg = (left_g, right_g)[p]
        landed(sg.at[gg, p], sg_s, sg_r.at[p], at_g(d))
        send(sg.at[gg, p], sg.at[gg, p], sg_s, sg_r.at[2], at_g(d))

    spread_on(0)
    second_leg(0)
    first_leg(1)
    spread_on(1)
    for p in range(2):
        split_solved(g, p)
        split_solved((left_g, right_g)[p], p)
    landed(sg.at[pl.ds(0, 2)], sg_s, sg_r.at[2], at_g(1))
    for p in range(2):
        split_solved((right_g, left_g)[p], p)
        split_solved(far_g, p)

    def tile_step(i, carry):
        def turn(n, inner):
            p = n // Q
            keep = jnp.where((i == 0) & (g == 0) & (row <= p), 0.0, 1.0).astype(F32)
            part = lg[i // 2, p, n % Q, :, :, pl.ds(pl.multiple_of((i % 2) * NB, NB), NB)].reshape(4 * 32, NB)
            hi, lo = split(part.T * keep)
            at = pl.ds(pl.multiple_of(n * 128, 128), 128)
            lh[:, at] = hi
            ll[:, at] = lo
            return inner

        lax.fori_loop(0, 2 * Q, turn, 0)

        def dest_step(m, inner):
            d = (m + 2) % Q
            gg = (g + d) % Q
            a, b = lh[...], sh[gg]
            acc = jnp.dot(a, b, preferred_element_type=F32)
            acc += jnp.dot(a, sl[gg], preferred_element_type=F32)
            acc += jnp.dot(ll[...], b, preferred_element_type=F32)

            @pl.when(d != 0)
            def _():
                n = Q * d - Q + i
                rhs_v[n] = acc
                send(rhs_v.at[n], upd.at[Q * g + i], u_s, u_r, (row, col_of(gg, o)))

            @pl.when(d == 0)
            def _():
                upd[Q * g + i] = acc

            return inner

        lax.fori_loop(0, Q, dest_step, 0)
        return carry

    tbv_in = pltpu.make_async_copy(tbv_hbm, tbv, loc.at[0])
    tbv_in.start()
    all_legs(0)
    lax.fori_loop(0, 1, tile_step, 0)
    second_leg(1)
    lax.fori_loop(1, 2, tile_step, 0)
    all_legs(1)
    lax.fori_loop(2, Q, tile_step, 0)

    tbv_in.wait()
    ids = tbv[...]
    every = lax.broadcasted_iota(jnp.int32, (TILES, ROWS * TILES), 1)
    want = lax.broadcasted_iota(jnp.int32, (TILES, ROWS * TILES), 0) * ROWS + row
    where_is = jnp.sum(jnp.where(ids == want, every, 0), axis=1, keepdims=True)
    before = (every < where_is) & (ids % ROWS == row)
    count = jnp.sum(before.astype(jnp.int32), axis=1, keepdims=True)
    count = jnp.broadcast_to(count, (TILES, ROWS * TILES))
    placing[...] = count

    own_t.wait()
    landed(send_v.at[pl.ds(0, TILES - 2)], az_s, az_r, sibling)
    left_here(send_v.at[pl.ds(0, TILES - 2)], az_s)
    left_here(send_v.at[pl.ds(0, 15)], lo_s)
    left_here(b1.at[0, pl.ds(0, Q - 1)], b1g_s)
    left_here(send_v.at[pl.ds(0, 9)], sg_s)

    @pl.when(row == 1)
    def _():
        left_here(send_v.at[0, pl.ds(0, 32 * (ROWS - 1))], b1z_s)

    left_here(rhs_v.at[pl.ds(0, 3 * Q)], u_s)
    landed(rhs_v.at[pl.ds(0, 3 * Q)], u_s, u_r, at_g(1))


def finish_body(placing, recv, upd, solved, out, solved_out, stage, sems, sol_sem):
    sol = pltpu.make_async_copy(solved, solved_out, sol_sem)
    sol.start()
    depth = stage.shape[0]
    places = [placing[b, 0] for b in range(TILES)]

    def put(b):
        return pltpu.make_async_copy(stage.at[b % depth], out.at[b], sems.at[b % depth])

    for b in range(TILES):
        if b >= depth:
            put(b - depth).wait()
        stage[b % depth] = recv[places[b]] - upd[b]
        put(b).start()
    for b in range(TILES - depth, TILES):
        put(b).wait()
    sol.wait()


def shards(rhs_atlas, tile_block, panels, diag_inverse):
    dma = pltpu.SemaphoreType.DMA
    hbm = pl.BlockSpec(memory_space=pltpu.HBM)
    vmem = pl.BlockSpec(memory_space=pltpu.VMEM)
    tiles = (TILES, NB, W)
    recv, upd, solved, placing = pl.pallas_call(
        exchange,
        out_shape=(
            pltpu.VMEM(tiles, F32),
            pltpu.VMEM(tiles, F32),
            pltpu.VMEM((2, NB, W), F32),
            pltpu.VMEM((TILES, ROWS * TILES), jnp.int32),
        ),
        in_specs=[hbm] * 5,
        out_specs=(vmem, vmem, vmem, vmem),
        scratch_shapes=[
            pltpu.VMEM(tiles, F32),
            pltpu.VMEM(tiles, F32),
            pltpu.VMEM((2, 2, Q, Q, 32, HB), F32),
            pltpu.VMEM((Q, 2, NB, W), F32),
            pltpu.VMEM((Q, 2 * NB, W), BF16),
            pltpu.VMEM((Q, 2 * NB, W), BF16),
            pltpu.VMEM((NB, 2 * NB), BF16),
            pltpu.VMEM((NB, 2 * NB), BF16),
            pltpu.VMEM((2, NB, W), F32),
            pltpu.VMEM((2, W, W), F32),
            pltpu.VMEM((Q - 1, 2, W // Q, W), F32),
            pltpu.VMEM((2, NB, W), F32),
            pltpu.VMEM((Q, Q, 32, W), F32),
            pltpu.VMEM((2, NB, NB), F32),
            pltpu.VMEM((NB, W), F32),
            pltpu.SMEM((ROWS * TILES,), jnp.int32),
            pltpu.VMEM((1, ROWS * TILES), jnp.int32),
            pltpu.SMEM((TILES + 4,), jnp.int32),
            dma((5,)), dma(()), dma(()), dma(()), dma(()), dma(()), dma((2,)), dma(()), dma((2, 3)),
            dma(()), dma(()), dma(()), dma(()), dma(()), dma(()), dma(()), dma(()), dma(()),
            dma(()), dma((3,)), dma(()), dma(()),
        ],
        compiler_params=pltpu.CompilerParams(
            collective_id=0, has_side_effects=True, vmem_limit_bytes=44 * 1024 * 1024
        ),
        name="exchange",
    )(tile_block, tile_block.reshape(1, -1), rhs_atlas.reshape(tiles), panels, diag_inverse)

    trailing, solved = pl.pallas_call(
        finish_body,
        out_shape=(jax.ShapeDtypeStruct(tiles, F32), jax.ShapeDtypeStruct((2, NB, W), F32)),
        in_specs=[vmem, vmem, vmem, vmem],
        out_specs=(hbm, hbm),
        scratch_shapes=[pltpu.VMEM((8, NB, W), F32), dma((8,)), dma(())],
        compiler_params=pltpu.CompilerParams(vmem_limit_bytes=6 * 1024 * 1024),
        name="finish",
    )(placing, recv, upd, solved)
    return solved, trailing.reshape(TILES * NB, W)


def solution(mesh):
    placed = (P("row", "col"), P(), P(None, "col", "row"), P())
    return jax.shard_map(
        shards,
        mesh=mesh,
        in_specs=placed,
        out_specs=(P(None, None, "col"), P("row", "col")),
        check_vma=False,
    )
```
